128 devices in a mesh: dp: 4 (over z), row: 8 (over x_lo, y), col: 4 (over x_hi, core).
Axes of the slice: x: 4 (x_hi: 2, x_lo: 2; x = x_hi * 2 + x_lo), y: 4, z: 4, core: 2. Of those that a mesh axis runs over, the one named last changes fastest.
Arguments:
- tokens: bfloat16 [32768, 6144], P(('dp', 'row', 'col')), may hold values from -60 to 60
- grads: bfloat16 [32768, 24576], P(('dp', 'row', 'col')), may hold values from -2 to 2
- weight_grad: bfloat16 [6144, 24576], P('row', ('dp', 'col')), may hold values from -0.5 to 0.5
Outputs:
- update: bfloat16 [6144, 24576], P('row', ('dp', 'col'))
The draws below stay inside these ranges and needn't reach their ends.
All inputs are finite; a program needn't handle non-finite values.
Results may differ from the reference program's by a relative error of at most 0.00065.
The reference program's roundings to bfloat16 on the way (of `inverse_in`, `inverse_out` and `left`) count: a program that leaves them out, or rounds other values in their place, can miss the bound.
Values may be sent and summed in bfloat16 or wider, within the bound.
A program may use at most 192 MiB of HBM per device.

```python
import math
import jax
import jax.numpy as jnp
from jax import lax

D = 6144
F = 24576
BLOCK = 192
STEPS = 3
TOKENS = 32768


def scaled_field(key, rows, cols, base, row_trend, col_trend, loose_columns):
    keys = jax.random.split(key, 5)
    row_pos = jnp.arange(rows, dtype=jnp.float32) / rows
    col_pos = jnp.arange(cols, dtype=jnp.float32) / cols
    row_scale = 10.0 ** (row_trend * row_pos) * jnp.exp(jax.random.uniform(keys[0], (rows,), jnp.float32, -0.35, 0.35))
    if loose_columns:
        col_scale = jnp.exp(jax.random.uniform(keys[1], (cols,), jnp.float32, jnp.log(0.3), jnp.log(3.0)))
    else:
        col_scale = 10.0 ** (col_trend * col_pos) * jnp.exp(jax.random.uniform(keys[1], (cols,), jnp.float32, -0.35, 0.35))
    noise = jax.random.truncated_normal(keys[4], -4.0, 4.0, (rows, cols), jnp.float32)
    return base * noise * row_scale[:, None] * col_scale[None, :]


def draw_tokens(key, part):
    return scaled_field(jax.random.fold_in(key, 11), TOKENS, D, 1.0 / 3.0, 1.0, 0.0, True).astype(jnp.bfloat16)


def draw_grads(key, part):
    base = 0.02 / 3.0
    return scaled_field(jax.random.fold_in(key, 23), TOKENS, F, base, 1.0, 0.0, True).astype(jnp.bfloat16)


def draw_weight_grad(key, part):
    base = 0.005
    return scaled_field(jax.random.fold_in(key, 37), D, F, base, 0.5, 0.5, False).astype(jnp.bfloat16)


def setup_inputs(seed: int = 0) -> dict:
    splits = jax.random.split(jax.random.key(seed), 4)
    return {
        "tokens": draw_tokens(jax.random.fold_in(splits[3], 71), 0),
        "grads": draw_grads(jax.random.fold_in(splits[3], 71), 0),
        "weight_grad": draw_weight_grad(jax.random.fold_in(splits[3], 71), 0),
    }


epsilon = 1e-06
damping = 0.01
trust_radius = 0.05
highest = lax.Precision.HIGHEST

def newton_inverse(blocks, shift):
    size = blocks.shape[-1]
    identity = jnp.eye(size, dtype=jnp.float32)
    matrix = blocks + shift * identity
    frobenius = jnp.sqrt(lax.optimization_barrier(jnp.sum(matrix * matrix, axis=(1, 2))))
    iterate = identity[None, :, :] / frobenius[:, None, None]
    for sweep in range(STEPS):
        product = jnp.einsum('nij,njk->nik', matrix, iterate, precision=highest)
        iterate = jnp.einsum('nij,njk->nik', iterate, 2.0 * identity - product, precision=highest)
    return iterate.astype(jnp.bfloat16)

def covariance(data):
    total = data.shape[0]
    count_blocks = data.shape[1] // BLOCK
    rows_step = math.gcd(total, 1024)

    def accumulate(index, summed):
        piece = lax.dynamic_slice_in_dim(data, index * rows_step, rows_step, 0)
        piece = piece.astype(jnp.float32).reshape(rows_step, count_blocks, BLOCK)
        return summed + jnp.einsum('tai,taj->aij', piece, piece, precision=highest)
    start = jnp.zeros((count_blocks, BLOCK, BLOCK), jnp.float32)
    return lax.fori_loop(0, total // rows_step, accumulate, start) / total

def block_trace(blocks):
    return jnp.sum(jnp.diagonal(blocks, axis1=1, axis2=2))

def reference(tokens, grads, weight_grad):
    cov_in = covariance(tokens)
    cov_out = covariance(grads)
    trace_in = block_trace(cov_in)
    trace_out = block_trace(cov_out)
    ratio = jnp.sqrt((trace_in / D + epsilon) / (trace_out / F + epsilon))
    damp_root = math.sqrt(damping)
    inverse_in = newton_inverse(cov_in, ratio * damp_root)
    inverse_out = newton_inverse(cov_out, damp_root / ratio)
    shaped = weight_grad.astype(jnp.float32).reshape(D // BLOCK, BLOCK, F)
    left = jnp.einsum('aij,ajc->aic', inverse_in.astype(jnp.float32), shaped, precision=highest)
    left = left.reshape(D, F).astype(jnp.bfloat16)
    natural = jnp.einsum('rkj,kji->rki', left.astype(jnp.float32).reshape(D, F // BLOCK, BLOCK), inverse_out.astype(jnp.float32), precision=highest).reshape(D, F)
    alignment = jnp.sum(natural * weight_grad.astype(jnp.float32))
    return (natural * jnp.sqrt(trust_radius * D * F / alignment)).astype(jnp.bfloat16)
```

```python
import functools
import math

import jax
import jax.numpy as jnp
from jax import lax
from jax.experimental import pallas as pl
from jax.experimental.pallas import tpu as pltpu
from jax.sharding import PartitionSpec as P

D = 6144
F = 24576
BLOCK = 192
TOKENS = 32768
EPSILON = 1e-06
DAMP_ROOT = math.sqrt(0.01)
TRUST_RADIUS = 0.05

PAIR = 2 * BLOCK
LOCAL = 256
IN_PAIRS = 8
OUT_PAIRS = 32
SUB_IN = 16
SUB_OUT = 64
ROWS = 768
COLS = 1536
MESH = pl.DeviceIdType.MESH
f32 = jnp.float32
bf16 = jnp.bfloat16


def mul(a, n):
    return pl.multiple_of(a, n)


def dot0(a, b):
    return lax.dot_general(a, b, (((0,), (0,)), ((), ())), preferred_element_type=f32)


def pair_pieces(data):
    d1 = dot0(data[:, 0:256], data[:, 0:256])
    d2 = dot0(data[:, 128:384], data[:, 256:384])
    low = lax.broadcasted_iota(jnp.int32, (64, 128), 1) < 64
    a = d1[0:128, 0:128]
    mid = d1[128:256, 128:256]
    b = d1[128:192, 0:128]
    even = (jnp.where(low, a[0:64], a[64:128]), jnp.where(low, mid[0:64], a[0:64]), b)
    a2 = d2[128:256]
    b2 = d2[64:128]
    odd = (jnp.where(low, a2[0:64], a2[64:128]), jnp.where(low, a2[64:128], mid[64:128]), b2)
    return even, odd


def pair_trace(even, odd):
    row = lax.broadcasted_iota(jnp.int32, (64, 128), 0)
    lane = lax.broadcasted_iota(jnp.int32, (64, 128), 1)
    first = lane == row
    second = lane == row + 64
    zero = jnp.zeros((64, 128), f32)
    total = jnp.where(first | second, even[0] + odd[0], zero)
    return total + jnp.where(first, even[1], zero) + jnp.where(second, odd[1], zero)


def newton(p0, p1, p2, parity, shift, u_ref):
    low = lax.broadcasted_iota(jnp.int32, (64, 128), 1) < 64
    even = parity == 0
    zero = jnp.zeros((64, 128), f32)
    u_ref[0:64, 0:128] = jnp.where(even, jnp.where(low, p0, p1), zero)
    u_ref[0:64, 128:256] = zero
    u_ref[64:128, 0:128] = jnp.where(low, zero, jnp.where(even, p0, p1))
    u_ref[64:128, 128:256] = jnp.where(even, zero, p2)
    u_ref[128:192, 0:128] = jnp.where(even, p2, zero)
    u_ref[128:192, 128:256] = jnp.where(low, jnp.where(even, p1, p0), zero)
    u_ref[192:256, 0:128] = zero
    u_ref[192:256, 128:256] = jnp.where(even, zero, jnp.where(low, p1, p0))
    u = u_ref[...]
    row = lax.broadcasted_iota(jnp.int32, (256, 256), 0)
    col = lax.broadcasted_iota(jnp.int32, (256, 256), 1)
    same = lax.div(row, 64) == lax.div(col, 64)
    valid = jnp.where(even, (row < BLOCK).astype(f32), (row >= 64).astype(f32))
    eye = jnp.where(row == col, valid, 0.0)
    matrix = u + jnp.where(same, 0.0, u.T) + shift * eye
    norm = jnp.sqrt(jnp.sum(jnp.sum(matrix * matrix, axis=1, keepdims=True), axis=0, keepdims=True))
    scale = 1.0 / norm
    dot = functools.partial(jnp.dot, precision=lax.Precision.HIGHEST, preferred_element_type=f32)
    r1 = eye - matrix * scale
    r2 = dot(r1, r1)
    r3 = dot(r1, r2)
    r4 = dot(r2, r2)
    low_sum = eye + r1 + r2 + r3
    return (scale * (low_sum + dot(low_sum, r4))).astype(bf16)


def kernel(
    tok, grd, wgt, out,
    tbuf, gbuf, wbuf, left, nat, ai, ao,
    ri0, ri1, ri2, ro0, ro1, ro2,
    inp, invi, invo, u_ref, tr_acc, al_acc, ar1, ar2,
    tsem, gsem, tss, tsr, gss, gsr, wsem, osem,
    nss, nsr, gs, gr,
):
    z = lax.axis_index("dp")
    row = lax.axis_index("row")
    col = lax.axis_index("col")
    xl = lax.div(row, 4)
    y = lax.rem(row, 4)
    xh = lax.div(col, 2)
    c = lax.rem(col, 2)
    x = xh * 2 + xl
    other = 1 - c
    pos = (x, y, z)

    def dev(xx, yy, zz, cc):
        return (zz, lax.rem(xx, 2) * 4 + yy, lax.div(xx, 2) * 2 + cc)

    def shifted(axis, delta):
        p = list(pos)
        p[axis] = lax.rem(p[axis] + delta, 4)
        return dev(*p, c)

    def remote(src, dst, ss, rs, device):
        pltpu.make_async_remote_copy(
            src_ref=src, dst_ref=dst, send_sem=ss, recv_sem=rs, device_id=device, device_id_type=MESH
        ).start()

    def wait(ref, sem):
        pltpu.make_async_copy(ref, ref, sem).wait()

    plane = []
    for j in range(1, 8):
        i = lax.rem(x * 2 + c + j, 8)
        plane.append(dev(lax.div(i, 2), y, z, lax.rem(i, 2)))
    sheet = []
    for j in range(1, 16):
        i = lax.rem(y * 4 + z + j, 16)
        sheet.append(dev(x, lax.div(i, 4), lax.rem(i, 4), c))
    diagonal = [dev(xh * 2 + 1 - xl, lax.rem(y + j, 4), z, c) for j in range(1, 4)]

    def tok_lanes(i, core):
        return pl.ds(mul((2 * i + core) * PAIR, 128), PAIR)

    def out_place(i):
        dz = lax.rem(2 + 3 * lax.div(i, 8), 4)
        dx = lax.rem(2 + 3 * lax.rem(lax.div(i, 2), 4), 4)
        yh = lax.rem(lax.div(y, 2) + 1 + lax.rem(i, 2), 2)
        return lax.rem(x + dx, 4), yh, lax.rem(z + dz, 4)

    def grd_lanes(i, core):
        xx, yh, zz = out_place(i)
        pair = (zz * 4 + lax.div(xx, 2) * 2 + core) * 4 + lax.rem(xx, 2) * 2 + yh
        return pl.ds(mul(pair * PAIR, 128), PAIR)

    @pl.loop(0, IN_PAIRS)
    def _(i):
        pltpu.make_async_copy(tok.at[:, tok_lanes(i, c)], tbuf.at[i, 0:LOCAL], tsem.at[i]).start()

    @pl.loop(0, OUT_PAIRS)
    def _(i):
        pltpu.make_async_copy(grd.at[:, grd_lanes(i, c)], gbuf.at[i, 0:LOCAL], gsem.at[i]).start()

    pltpu.make_async_copy(wgt, wbuf, wsem).start()

    for k in range(8):
        start = 192 if k % 2 == 0 else 0
        invo[k, start : start + 64] = jnp.zeros((64, 256), bf16)
    tr_acc[...] = jnp.zeros_like(tr_acc)

    barrier = pltpu.get_barrier_semaphore()
    peers = plane + sheet + diagonal
    for device in peers:
        pl.semaphore_signal(barrier, inc=1, device_id=device, device_id_type=MESH)
    pl.semaphore_wait(barrier, len(peers))

    partner = dev(x, y, z, other)

    @pl.loop(0, IN_PAIRS)
    def _(i):
        remote(tok.at[:, tok_lanes(i, other)], tbuf.at[i, LOCAL:], tss.at[0], tsr.at[i], partner)

    @pl.loop(0, OUT_PAIRS)
    def _(i):
        remote(grd.at[:, grd_lanes(i, other)], gbuf.at[i, LOCAL:], gss.at[0], gsr.at[i], partner)

    def index(p, xx, yy, zz):
        t = (xx, yy, zz)
        return t[p] * 16 + t[(p + 1) % 3] * 4 + t[(p + 2) % 3]

    bufs = (ai, ao)
    recvs = ((ri0, ri1, ri2), (ro0, ro1, ro2))
    subs = (SUB_IN, SUB_OUT)

    def chunk(net, stage):
        return (16, 4, 1)[stage] * subs[net]

    def base(net, p, stage):
        b = 0
        for s in range(stage):
            b = b + pos[(p + s) % 3] * chunk(net, s)
        return b

    def ring(net, stage, p):
        n = chunk(net, stage)
        h = n // 2
        b = base(net, p, stage)
        axis = (p + stage) % 3
        me = pos[axis]
        buf = bufs[net].at[p]
        recv = recvs[net][stage].at[p]

        def part(step, offset, rows):
            return pl.ds(mul(b + lax.rem(me + step, 4) * n + offset, 8), rows)

        def send(direction, kind, step, offset):
            at = 0 if kind == 0 else h + offset
            remote(
                buf.at[part(step, offset, h)], recv.at[direction, pl.ds(at, h)],
                nss.at[net, stage, p], nsr.at[net, stage, p, 2 * kind + direction],
                shifted(axis, 3 if direction else 1),
            )

        def got(direction, kind, offset):
            at = 0 if kind == 0 else h + offset
            wait(recv.at[direction, pl.ds(at, h)], nsr.at[net, stage, p, 2 * kind + direction])

        def issue():
            send(0, 0, 2, 0)
            send(1, 0, 2, h)
            send(0, 1, 1, h)
            send(1, 1, 3, 0)

        def relay():
            for direction, step, offset in ((0, 1, 0), (1, 3, h)):
                got(direction, 0, 0)
                rows = part(step, offset, h)
                buf[rows] = buf[rows] + recv[direction, 0:h]
                send(direction, 2, step, offset)

        def final():
            got(0, 1, h)
            got(1, 1, 0)
            got(0, 2, 0)
            got(1, 2, h)
            rows = part(0, 0, n)
            buf[rows] = buf[rows] + recv[0, h : h + n] + recv[1, h : h + n]

        return issue, relay, final

    @pl.loop(0, IN_PAIRS)
    def _(i):
        wait(tbuf.at[i, 0:LOCAL], tsem.at[i])
        wait(tbuf.at[i, LOCAL:], tsr.at[i])
        pieces = pair_pieces(tbuf[i])
        tr_acc[1] = tr_acc[1] + pair_trace(*pieces)
        for e in range(2):
            xx = 2 * e + lax.div(i, 4)
            for p in range(3):
                for zz in range(4):
                    at = index(p, xx, lax.rem(i, 4), zz) * SUB_IN
                    ai[p, pl.ds(mul(at, SUB_IN), SUB_IN)] = pieces[e][p][zz * 16 : zz * 16 + 16]

    in_rings = [[ring(0, s, p) for p in range(3)] for s in range(3)]
    out_rings = [[ring(1, s, p) for p in range(3)] for s in range(3)]
    for p in range(3):
        in_rings[0][p][0]()

    half = 8 * SUB_OUT

    @pl.loop(0, OUT_PAIRS)
    def _(i):
        xx, yh, zz = out_place(i)
        wait(gbuf.at[i, 0:LOCAL], gsem.at[i])
        wait(gbuf.at[i, LOCAL:], gsr.at[i])
        pieces = pair_pieces(gbuf[i])
        tr_acc[0] = tr_acc[0] + pair_trace(*pieces)
        for e in range(2):
            place = (xx, 2 * yh + e, zz)
            for p in range(3):
                number = index(p, *place)
                rows = pl.ds(mul(number * SUB_OUT, SUB_OUT), SUB_OUT)
                ao[p, rows] = pieces[e][p]
                sub = lax.rem(number, 16)
                d = lax.rem(place[p] - pos[p] + 4, 4)
                h = lax.div(sub, 8)
                far = (1 - lax.rem(d, 2)) * lax.div(d, 2)
                go = far + lax.rem(d, 2) * lax.rem(lax.div(d, 2) + h, 2)
                direction = far * h + (1 - far) * (1 - h)
                at = far * lax.rem(sub, 8) * SUB_OUT + (1 - far) * (half + sub * SUB_OUT)

                @pl.when(go == 1)
                def _():
                    remote(
                        ao.at[p, rows], ro0.at[p, direction, pl.ds(mul(at, SUB_OUT), SUB_OUT)],
                        nss.at[1, 0, p], nsr.at[1, 0, p, 2 * (1 - far) + direction],
                        shifted(p, 1 + 2 * direction),
                    )

    def reduce_start(use, value):
        mine = x * 2 + c
        ar1[use, mine] = value
        for device in plane:
            remote(ar1.at[use, mine], ar1.at[use, mine], gs.at[use], gr.at[use], device)

    def reduce_middle(use):
        wait(ar1.at[use, 0:7], gr.at[use])
        mine = y * 4 + z
        ar2[use, mine] = jnp.sum(ar1[use], axis=0)
        for device in sheet:
            remote(ar2.at[use, mine], ar2.at[use, mine], gs.at[2 + use], gr.at[2 + use], device)

    def reduce_end(use):
        wait(ar2.at[use, 0:15], gr.at[2 + use])
        return jnp.sum(ar2[use], axis=0)

    def total(value):
        return jnp.sum(jnp.sum(value, axis=1, keepdims=True), axis=0, keepdims=True)

    t_out = jnp.sum(tr_acc[0].reshape(16, 4, 128), axis=0)
    t_in = jnp.sum(tr_acc[1].reshape(16, 4, 128), axis=0)
    reduce_start(0, jnp.concatenate([t_out, t_in], axis=0))

    for p in (2, 0, 1):
        in_rings[0][p][1]()
    for p in (2, 0, 1):
        out_rings[0][p][1]()
    reduce_middle(0)
    for s in range(1, 3):
        for p in range(3):
            in_rings[s - 1][p][2]()
            in_rings[s][p][0]()
        for p in range(3):
            in_rings[s][p][1]()
    for p in range(3):
        in_rings[2][p][2]()

    quarter = pl.ds(mul(z * SUB_IN, SUB_IN), SUB_IN)
    for p in range(3):
        inp[p, quarter] = ai[p, pl.ds(mul(index(p, x, y, z) * SUB_IN, SUB_IN), SUB_IN)]
    for j in range(1, 4):
        remote(inp.at[:, quarter], inp.at[:, quarter], gs.at[4], gr.at[4], shifted(2, j))

    traces = reduce_end(0)
    inverse_count = 1.0 / TOKENS
    trace_out = total(traces[0:4]) * inverse_count
    trace_in = total(traces[4:8]) * inverse_count
    ratio = jnp.sqrt((trace_in / D + EPSILON) / (trace_out / F + EPSILON))

    wait(inp.at[:, 0:48], gr.at[4])
    x_in = newton(
        inp[0] * inverse_count, inp[1] * inverse_count, inp[2] * inverse_count, xh, ratio * DAMP_ROOT, u_ref
    )
    slot = c * 2 + xh
    invi[slot] = x_in
    span = pl.ds(mul(xh * 64, 64), BLOCK)
    for j in range(1, 4):
        i = lax.rem(col + j, 4)
        device = dev(lax.div(i, 2) * 2 + xl, y, z, lax.rem(i, 2))
        remote(invi.at[slot, span], invi.at[slot, span], gs.at[5], gr.at[5], device)

    wait(wbuf, wsem)
    wait(invi.at[0:3, 0:BLOCK], gr.at[5])

    @pl.loop(0, 4)
    def _(n):
        lanes = pl.ds(mul(n * PAIR, 128), PAIR)
        for q in range(2):
            at = q * PAIR
            first = jnp.dot(
                invi[2 * q, 0:192], wbuf[at : at + 256, lanes], preferred_element_type=f32
            )
            second = jnp.dot(
                invi[2 * q + 1, 64:256], wbuf[at + 128 : at + 384, lanes], preferred_element_type=f32
            )
            left[at : at + 192, lanes] = first.astype(bf16)
            left[at + 192 : at + 384, lanes] = second.astype(bf16)

    for s in range(1, 3):
        for p in (2, 0, 1):
            out_rings[s - 1][p][2]()
            out_rings[s][p][0]()
        for p in (2, 0, 1):
            out_rings[s][p][1]()
    for p in (2, 0, 1):
        out_rings[2][p][2]()

    own = [
        ao[p, pl.ds(mul(index(p, x, y, z) * SUB_OUT, SUB_OUT), SUB_OUT)] * inverse_count for p in range(3)
    ]
    parity = lax.rem(y, 2)
    x_out = newton(own[0], own[1], own[2], parity, DAMP_ROOT / ratio, u_ref)
    invo[row] = x_out
    span_out = pl.ds(mul(parity * 64, 64), BLOCK)
    for j in range(1, 8):
        i = lax.rem(row + j, 8)
        device = (z, i, col)
        remote(invo.at[row, span_out], invo.at[row, span_out], gs.at[6], gr.at[6], device)
    al_acc[...] = jnp.zeros_like(al_acc)
    wait(invo.at[0:7, 0:BLOCK], gr.at[6])

    @pl.loop(0, 12)
    def _(n):
        q = lax.div(n, 3)
        rows = pl.ds(mul(lax.rem(n, 3) * 256, 256), 256)
        at = q * PAIR
        lanes = pl.ds(mul(at, 128), PAIR)
        first = jnp.dot(
            left[rows, pl.ds(mul(at, 128), 256)], invo[2 * q], preferred_element_type=f32
        )
        second = jnp.dot(
            left[rows, pl.ds(mul(at + 128, 128), 256)], invo[2 * q + 1], preferred_element_type=f32
        )
        natural = jnp.concatenate(
            [first[:, 0:128], first[:, 128:256] + second[:, 0:128], second[:, 128:256]], axis=1
        )
        nat[rows, lanes] = natural
        product = (natural * wbuf[rows, lanes].astype(f32)).reshape(32, 8, PAIR).sum(axis=0)
        al_acc[...] = al_acc[...] + product[:, 0:128] + product[:, 128:256] + product[:, 256:384]

    reduce_start(1, al_acc[...])
    reduce_middle(1)
    alignment = total(reduce_end(1))
    factor = jnp.sqrt(TRUST_RADIUS * D * F / alignment)

    @pl.loop(0, 6)
    def _(n):
        rows = pl.ds(mul(n * 128, 128), 128)
        wbuf[rows] = (nat[rows] * factor).astype(bf16)
        pltpu.make_async_copy(wbuf.at[rows], out.at[rows], osem).start()

    wait(tbuf.at[:, LOCAL:], tss.at[0])
    wait(gbuf.at[:, LOCAL:], gss.at[0])
    for net in range(2):
        for s in range(3):
            for p in range(3):
                wait(recvs[net][s].at[p], nss.at[net, s, p])
    for use in range(2):
        wait(ar1.at[use, 0:7], gs.at[use])
        wait(ar2.at[use, 0:15], gs.at[2 + use])
    wait(inp.at[:, 0:48], gs.at[4])
    wait(invi.at[0:3, 0:BLOCK], gs.at[5])
    wait(invo.at[0:7, 0:BLOCK], gs.at[6])
    wait(wbuf, osem)


def on_device(tokens, grads, weight_grad):
    dma = pltpu.SemaphoreType.DMA
    any_space = pl.BlockSpec(memory_space=pl.ANY)
    vmem = pltpu.VMEM

    def received(sub):
        return [vmem((3, 2, 24 * sub // 4**s, 128), f32) for s in range(3)]

    return pl.pallas_call(
        kernel,
        out_shape=jax.ShapeDtypeStruct((ROWS, COLS), bf16),
        in_specs=[any_space] * 3,
        out_specs=any_space,
        scratch_shapes=[
            vmem((IN_PAIRS, 2 * LOCAL, PAIR), bf16),
            vmem((OUT_PAIRS, 2 * LOCAL, PAIR), bf16),
            vmem((ROWS, COLS), bf16),
            vmem((ROWS, COLS), bf16),
            vmem((ROWS, COLS), f32),
            vmem((3, 64 * SUB_IN, 128), f32),
            vmem((3, 64 * SUB_OUT, 128), f32),
            *received(SUB_IN),
            *received(SUB_OUT),
            vmem((3, 64, 128), f32),
            vmem((4, 256, 256), bf16),
            vmem((8, 256, 256), bf16),
            vmem((256, 256), f32),
            vmem((2, 64, 128), f32),
            vmem((8, 128), f32),
            vmem((2, 8, 8, 128), f32),
            vmem((2, 16, 8, 128), f32),
            dma((IN_PAIRS,)),
            dma((OUT_PAIRS,)),
            dma((1,)),
            dma((IN_PAIRS,)),
            dma((1,)),
            dma((OUT_PAIRS,)),
            dma(()),
            dma(()),
            dma((2, 3, 3)),
            dma((2, 3, 3, 6)),
            dma((7,)),
            dma((7,)),
        ],
        compiler_params=pltpu.CompilerParams(
            collective_id=0, has_side_effects=True, vmem_limit_bytes=60 * 1024 * 1024
        ),
        name="kfac_step",
    )(tokens, grads, weight_grad)


def solution(mesh):
    every = P(("dp", "row", "col"), None)
    weight = P("row", ("dp", "col"))
    return jax.shard_map(
        on_device, mesh=mesh, in_specs=(every, every, weight), out_specs=weight, check_vma=False
    )
```

```python
import functools
import math

import jax
import jax.numpy as jnp
from jax import lax
from jax.experimental import pallas as pl
from jax.experimental.pallas import tpu as pltpu
from jax.sharding import PartitionSpec as P

D = 6144
F = 24576
BLOCK = 192
TOKENS = 32768
EPSILON = 1e-06
DAMP_ROOT = math.sqrt(0.01)
TRUST_RADIUS = 0.05

PAIR = 2 * BLOCK
LOCAL = 256
IN_PAIRS = 8
OUT_PAIRS = 32
SUB_IN = 16
SUB_OUT = 64
ROWS = 768
COLS = 1536
MESH = pl.DeviceIdType.MESH
f32 = jnp.float32
bf16 = jnp.bfloat16


def mul(a, n):
    return pl.multiple_of(a, n)


def dot0(a, b):
    return lax.dot_general(a, b, (((0,), (0,)), ((), ())), preferred_element_type=f32)


def pair_pieces(data):
    d1 = dot0(data[:, 0:256], data[:, 0:256])
    d2 = dot0(data[:, 128:384], data[:, 256:384])
    low = lax.broadcasted_iota(jnp.int32, (64, 128), 1) < 64
    a = d1[0:128, 0:128]
    mid = d1[128:256, 128:256]
    b = d1[128:192, 0:128]
    even = (jnp.where(low, a[0:64], a[64:128]), jnp.where(low, mid[0:64], a[0:64]), b)
    a2 = d2[128:256]
    b2 = d2[64:128]
    odd = (jnp.where(low, a2[0:64], a2[64:128]), jnp.where(low, a2[64:128], mid[64:128]), b2)
    return even, odd


def pair_trace(even, odd):
    row = lax.broadcasted_iota(jnp.int32, (64, 128), 0)
    lane = lax.broadcasted_iota(jnp.int32, (64, 128), 1)
    first = lane == row
    second = lane == row + 64
    zero = jnp.zeros((64, 128), f32)
    total = jnp.where(first | second, even[0] + odd[0], zero)
    return total + jnp.where(first, even[1], zero) + jnp.where(second, odd[1], zero)


def frame(p0, p1, p2, parity, u_ref):
    low = lax.broadcasted_iota(jnp.int32, (64, 128), 1) < 64
    even = parity == 0
    zero = jnp.zeros((64, 128), f32)
    u_ref[0:64, 0:128] = jnp.where(even, jnp.where(low, p0, p1), zero)
    u_ref[0:64, 128:256] = zero
    u_ref[64:128, 0:128] = jnp.where(low, zero, jnp.where(even, p0, p1))
    u_ref[64:128, 128:256] = jnp.where(even, zero, p2)
    u_ref[128:192, 0:128] = jnp.where(even, p2, zero)
    u_ref[128:192, 128:256] = jnp.where(low, jnp.where(even, p1, p0), zero)
    u_ref[192:256, 0:128] = zero
    u_ref[192:256, 128:256] = jnp.where(even, zero, jnp.where(low, p1, p0))
    u = u_ref[...]
    row = lax.broadcasted_iota(jnp.int32, (256, 256), 0)
    col = lax.broadcasted_iota(jnp.int32, (256, 256), 1)
    same = lax.div(row, 64) == lax.div(col, 64)
    return u + jnp.where(same, 0.0, u.T)


def newton(p0, p1, p2, parity, shift, u_ref):
    even = parity == 0
    row = lax.broadcasted_iota(jnp.int32, (256, 256), 0)
    col = lax.broadcasted_iota(jnp.int32, (256, 256), 1)
    valid = jnp.where(even, (row < BLOCK).astype(f32), (row >= 64).astype(f32))
    eye = jnp.where(row == col, valid, 0.0)
    matrix = frame(p0, p1, p2, parity, u_ref) + shift * eye
    norm = jnp.sqrt(jnp.sum(jnp.sum(matrix * matrix, axis=1, keepdims=True), axis=0, keepdims=True))
    scale = 1.0 / norm
    dot = functools.partial(jnp.dot, precision=lax.Precision.HIGHEST, preferred_element_type=f32)
    r1 = eye - matrix * scale
    r2 = dot(r1, r1)
    r3 = dot(r1, r2)
    r4 = dot(r2, r2)
    low_sum = eye + r1 + r2 + r3
    inv = scale * (low_sum + dot(low_sum, r4))
    low = lax.broadcasted_iota(jnp.int32, (64, 128), 1) < 64
    q0 = jnp.where(
        low,
        jnp.where(even, inv[0:64, 0:128], inv[128:192, 128:256]),
        jnp.where(even, inv[64:128, 0:128], inv[192:256, 128:256]),
    )
    q1 = jnp.where(
        low,
        jnp.where(even, inv[128:192, 128:256], inv[192:256, 128:256]),
        jnp.where(even, inv[0:64, 0:128], inv[64:128, 0:128]),
    )
    q2 = jnp.where(even, inv[128:192, 0:128], inv[64:128, 128:256])
    return q0.astype(bf16), q1.astype(bf16), q2.astype(bf16)


def kernel(
    tok, grd, wgt, out,
    tbuf, gbuf, wbuf, left, nat, ai, ao,
    ri0, ri1, ri2, ro0, ro1, ro2,
    inp, ini, ino, invi, invo, u_ref, tr_acc, al_acc, ar1, ar2,
    tsem, gsem, tss, tsr, gss, gsr, wsem,
    nss, nsr, gs, gr, orx,
):
    z = lax.axis_index("dp")
    row = lax.axis_index("row")
    col = lax.axis_index("col")
    xl = lax.div(row, 4)
    y = lax.rem(row, 4)
    xh = lax.div(col, 2)
    c = lax.rem(col, 2)
    x = xh * 2 + xl
    other = 1 - c
    pos = (x, y, z)

    def dev(xx, yy, zz, cc):
        return (zz, lax.rem(xx, 2) * 4 + yy, lax.div(xx, 2) * 2 + cc)

    def shifted(axis, delta):
        p = list(pos)
        p[axis] = lax.rem(p[axis] + delta, 4)
        return dev(*p, c)

    def remote(src, dst, ss, rs, device):
        pltpu.make_async_remote_copy(
            src_ref=src, dst_ref=dst, send_sem=ss, recv_sem=rs, device_id=device, device_id_type=MESH
        ).start()

    def wait(ref, sem):
        pltpu.make_async_copy(ref, ref, sem).wait()

    plane = []
    for j in range(1, 8):
        i = lax.rem(x * 2 + c + j, 8)
        plane.append(dev(lax.div(i, 2), y, z, lax.rem(i, 2)))
    sheet = []
    for j in range(1, 16):
        i = lax.rem(y * 4 + z + j, 16)
        sheet.append(dev(x, lax.div(i, 4), lax.rem(i, 4), c))
    diagonal = [dev(xh * 2 + 1 - xl, lax.rem(y + j, 4), z, c) for j in range(1, 4)]
    x_far, z_far = lax.rem(x + 2, 4), lax.rem(z + 2, 4)
    z_near = z + 1 - 2 * lax.rem(z, 2)
    corners = [dev(x_far, y, z, c), dev(x, y, z_far, c), dev(x_far, y, z_far, c)]
    cousins = [dev(x, y, z, other), dev(x, y, z_near, c), dev(x, y, z_near, other)]

    def tok_lanes(i, core):
        return pl.ds(mul((2 * i + core) * PAIR, 128), PAIR)

    def out_place(i):
        dz = lax.rem(2 + 3 * lax.div(i, 8), 4)
        dx = lax.rem(2 + 3 * lax.rem(lax.div(i, 2), 4), 4)
        yh = lax.rem(lax.div(y, 2) + 1 + lax.rem(i, 2), 2)
        return lax.rem(x + dx, 4), yh, lax.rem(z + dz, 4)

    def grd_lanes(i, core):
        xx, yh, zz = out_place(i)
        pair = (zz * 4 + lax.div(xx, 2) * 2 + core) * 4 + lax.rem(xx, 2) * 2 + yh
        return pl.ds(mul(pair * PAIR, 128), PAIR)

    @pl.loop(0, IN_PAIRS)
    def _(i):
        pltpu.make_async_copy(tok.at[:, tok_lanes(i, c)], tbuf.at[i, 0:LOCAL], tsem.at[i]).start()

    @pl.loop(0, OUT_PAIRS)
    def _(i):
        pltpu.make_async_copy(grd.at[:, grd_lanes(i, c)], gbuf.at[i, 0:LOCAL], gsem.at[i]).start()

    pltpu.make_async_copy(wgt, wbuf, wsem).start()

    tr_acc[...] = jnp.zeros_like(tr_acc)
    nat[...] = jnp.zeros_like(nat)

    barrier = pltpu.get_barrier_semaphore()
    peers = plane + sheet + diagonal + [corners[2], cousins[2]]
    for device in peers:
        pl.semaphore_signal(barrier, inc=1, device_id=device, device_id_type=MESH)
    pl.semaphore_wait(barrier, len(peers))

    partner = dev(x, y, z, other)

    @pl.loop(0, IN_PAIRS)
    def _(i):
        remote(tok.at[:, tok_lanes(i, other)], tbuf.at[i, LOCAL:], tss.at[0], tsr.at[i], partner)

    @pl.loop(0, OUT_PAIRS)
    def _(i):
        remote(grd.at[:, grd_lanes(i, other)], gbuf.at[i, LOCAL:], gss.at[0], gsr.at[i], partner)

    def index(p, xx, yy, zz):
        t = (xx, yy, zz)
        return t[p] * 16 + t[(p + 1) % 3] * 4 + t[(p + 2) % 3]

    bufs = (ai, ao)
    recvs = ((ri0, ri1, ri2), (ro0, ro1, ro2))
    subs = (SUB_IN, SUB_OUT)

    def chunk(net, stage):
        return (16, 4, 1)[stage] * subs[net]

    def base(net, p, stage):
        b = 0
        for s in range(stage):
            b = b + pos[(p + s) % 3] * chunk(net, s)
        return b

    def ring(net, stage, p):
        n = chunk(net, stage)
        h = n // 2
        b = base(net, p, stage)
        axis = (p + stage) % 3
        me = pos[axis]
        buf = bufs[net].at[p]
        recv = recvs[net][stage].at[p]

        def part(step, offset, rows):
            return pl.ds(mul(b + lax.rem(me + step, 4) * n + offset, 8), rows)

        def send(direction, kind, step, offset):
            at = 0 if kind == 0 else h + offset
            remote(
                buf.at[part(step, offset, h)], recv.at[direction, pl.ds(at, h)],
                nss.at[net, stage, p], nsr.at[net, stage, p, 2 * kind + direction],
                shifted(axis, 3 if direction else 1),
            )

        def got(direction, kind, offset):
            at = 0 if kind == 0 else h + offset
            wait(recv.at[direction, pl.ds(at, h)], nsr.at[net, stage, p, 2 * kind + direction])

        def issue():
            send(0, 0, 2, 0)
            send(1, 0, 2, h)
            send(0, 1, 1, h)
            send(1, 1, 3, 0)

        def relay():
            for direction, step, offset in ((0, 1, 0), (1, 3, h)):
                got(direction, 0, 0)
                rows = part(step, offset, h)
                buf[rows] = buf[rows] + recv[direction, 0:h]
                send(direction, 2, step, offset)

        def final():
            got(0, 1, h)
            got(1, 1, 0)
            got(0, 2, 0)
            got(1, 2, h)
            rows = part(0, 0, n)
            buf[rows] = buf[rows] + recv[0, h : h + n] + recv[1, h : h + n]

        return issue, relay, final

    @pl.loop(0, IN_PAIRS)
    def _(i):
        wait(tbuf.at[i, 0:LOCAL], tsem.at[i])
        wait(tbuf.at[i, LOCAL:], tsr.at[i])
        pieces = pair_pieces(tbuf[i])
        tr_acc[1] = tr_acc[1] + pair_trace(*pieces)
        for e in range(2):
            for p in range(3):
                for q in range(4):
                    xx = q // 2 * 2 + lax.div(i, 4)
                    at = index(p, xx, lax.rem(i, 4), q % 2 * 2 + e) * SUB_IN
                    ai[p, pl.ds(mul(at, SUB_IN), SUB_IN)] = pieces[e][p][q * 16 : q * 16 + 16]

    in_rings = [[ring(0, s, p) for p in range(3)] for s in range(3)]
    out_rings = [[ring(1, s, p) for p in range(3)] for s in range(3)]
    for p in range(3):
        in_rings[0][p][0]()

    half = 8 * SUB_OUT

    @pl.loop(0, OUT_PAIRS)
    def _(i):
        xx, yh, zz = out_place(i)
        @pl.when(i == 20)
        def _():
            for p in range(3):
                in_rings[0][p][1]()

        wait(gbuf.at[i, 0:LOCAL], gsem.at[i])
        wait(gbuf.at[i, LOCAL:], gsr.at[i])
        pieces = pair_pieces(gbuf[i])
        tr_acc[0] = tr_acc[0] + pair_trace(*pieces)
        for e in range(2):
            place = (xx, 2 * yh + e, zz)
            for p in range(3):
                number = index(p, *place)
                rows = pl.ds(mul(number * SUB_OUT, SUB_OUT), SUB_OUT)
                ao[p, rows] = pieces[e][p]
                sub = lax.rem(number, 16)
                d = lax.rem(place[p] - pos[p] + 4, 4)
                h = lax.div(sub, 8)
                far = (1 - lax.rem(d, 2)) * lax.div(d, 2)
                go = far + lax.rem(d, 2) * lax.rem(lax.div(d, 2) + h, 2)
                direction = far * h + (1 - far) * (1 - h)
                at = far * lax.rem(sub, 8) * SUB_OUT + (1 - far) * (half + sub * SUB_OUT)

                @pl.when(go == 1)
                def _():
                    remote(
                        ao.at[p, rows], ro0.at[p, direction, pl.ds(mul(at, SUB_OUT), SUB_OUT)],
                        nss.at[1, 0, p], nsr.at[1, 0, p, 2 * (1 - far) + direction],
                        shifted(p, 1 + 2 * direction),
                    )

    def reduce_start(use, value):
        mine = x * 2 + c
        ar1[use, mine] = value
        for device in plane:
            remote(ar1.at[use, mine], ar1.at[use, mine], gs.at[use], gr.at[use], device)

    def reduce_middle(use):
        wait(ar1.at[use, 0:7], gr.at[use])
        mine = y * 4 + z
        ar2[use, mine] = jnp.sum(ar1[use], axis=0)
        for device in sheet:
            remote(ar2.at[use, mine], ar2.at[use, mine], gs.at[2 + use], gr.at[2 + use], device)

    def reduce_end(use):
        wait(ar2.at[use, 0:15], gr.at[2 + use])
        return jnp.sum(ar2[use], axis=0)

    def total(value):
        return jnp.sum(jnp.sum(value, axis=1, keepdims=True), axis=0, keepdims=True)

    t_out = jnp.sum(tr_acc[0].reshape(16, 4, 128), axis=0)
    t_in = jnp.sum(tr_acc[1].reshape(16, 4, 128), axis=0)
    reduce_start(0, jnp.concatenate([t_out, t_in], axis=0))

    order = (2, 0, 1)

    def step(rings, stage, kind):
        for p in order:
            rings[stage][p][kind]()

    def advance(rings, stage):
        for p in order:
            rings[stage][p][2]()
            rings[stage + 1][p][0]()

    step(out_rings, 0, 1)
    advance(in_rings, 0)
    reduce_middle(0)
    step(in_rings, 1, 1)
    advance(out_rings, 0)
    advance(in_rings, 1)
    traces = reduce_end(0)
    inverse_count = 1.0 / TOKENS
    trace_out = total(traces[0:4]) * inverse_count
    trace_in = total(traces[4:8]) * inverse_count
    ratio = jnp.sqrt((trace_in / D + EPSILON) / (trace_out / F + EPSILON))
    step(out_rings, 1, 1)
    step(in_rings, 2, 1)
    advance(out_rings, 1)
    step(in_rings, 2, 2)

    quarter = pl.ds(mul((xh * 2 + lax.div(z, 2)) * SUB_IN, SUB_IN), SUB_IN)
    for p in range(3):
        inp[p, quarter] = ai[p, pl.ds(mul(index(p, x, y, z) * SUB_IN, SUB_IN), SUB_IN)]
    for device in corners:
        remote(inp.at[:, quarter], inp.at[:, quarter], gs.at[4], gr.at[4], device)

    step(out_rings, 2, 1)
    step(out_rings, 2, 2)

    own = [
        ao[p, pl.ds(mul(index(p, x, y, z) * SUB_OUT, SUB_OUT), SUB_OUT)] * inverse_count for p in range(3)
    ]
    for p, piece in enumerate(newton(*own, lax.rem(y, 2), DAMP_ROOT / ratio, u_ref)):
        ino[row, p] = piece
    for j in range(1, 8):
        i = lax.rem(row + j, 8)
        remote(ino.at[row], ino.at[row], gs.at[6], orx.at[row], (z, i, col))
    al_acc[...] = jnp.zeros_like(al_acc)

    wait(inp.at[:, 0:48], gr.at[4])
    slot = c * 2 + lax.rem(z, 2)
    mine = [inp[p] * inverse_count for p in range(3)]
    for p, piece in enumerate(newton(*mine, lax.rem(z, 2), ratio * DAMP_ROOT, u_ref)):
        ini[slot, p] = piece
    for device in cousins:
        remote(ini.at[slot], ini.at[slot], gs.at[5], gr.at[5], device)

    wait(wbuf, wsem)
    wait(ini.at[0:3], gr.at[5])

    @pl.loop(0, 4)
    def _(k):
        pieces = [ini[k, p].astype(f32) for p in range(3)]
        invi[k] = frame(*pieces, lax.rem(k, 2), u_ref).astype(bf16)

    @pl.loop(0, 4)
    def _(n):
        lanes = pl.ds(mul(n * PAIR, 128), PAIR)
        for q in range(2):
            at = q * PAIR
            first = jnp.dot(
                invi[2 * q, 0:192], wbuf[at : at + 256, lanes], preferred_element_type=f32
            )
            second = jnp.dot(
                invi[2 * q + 1, 64:256], wbuf[at + 128 : at + 384, lanes], preferred_element_type=f32
            )
            left[at : at + 192, lanes] = first.astype(bf16)
            left[at + 192 : at + 384, lanes] = second.astype(bf16)

    @pl.loop(0, 8)
    def _(j):
        m = lax.rem(j, 4)
        yy = lax.rem(y + m + lax.div(m, 2) * (5 - 2 * m), 4)
        k = lax.rem(xl + lax.div(j, 4), 2) * 4 + yy

        @pl.when(j > 0)
        def _():
            wait(ino.at[k], orx.at[k])

        pieces = [ino[k, p].astype(f32) for p in range(3)]
        invo[...] = frame(*pieces, lax.rem(k, 2), u_ref).astype(bf16)
        lanes = pl.ds(mul(lax.div(k, 2) * PAIR + lax.rem(k, 2) * 128, 128), 256)
        for n in range(3):
            rows = pl.ds(n * 256, 256)
            part = jnp.dot(left[rows, lanes], invo[...], preferred_element_type=f32)
            nat[rows, lanes] = nat[rows, lanes] + part
            product = (part * wbuf[rows, lanes].astype(f32)).reshape(32, 8, 256).sum(axis=0)
            al_acc[...] = al_acc[...] + product[:, 0:128] + product[:, 128:256]

    reduce_start(1, al_acc[...])
    reduce_middle(1)
    alignment = total(reduce_end(1))
    factor = jnp.sqrt(TRUST_RADIUS * D * F / alignment)
    out[...] = (nat[...] * factor).astype(bf16)

    wait(tbuf.at[:, LOCAL:], tss.at[0])
    wait(gbuf.at[:, LOCAL:], gss.at[0])
    for net in range(2):
        for s in range(3):
            for p in range(3):
                wait(recvs[net][s].at[p], nss.at[net, s, p])
    for use in range(2):
        wait(ar1.at[use, 0:7], gs.at[use])
        wait(ar2.at[use, 0:15], gs.at[2 + use])
    wait(inp.at[:, 0:48], gs.at[4])
    wait(ini.at[0:3], gs.at[5])
    wait(ino.at[0:7], gs.at[6])


def on_device(tokens, grads, weight_grad):
    dma = pltpu.SemaphoreType.DMA
    any_space = pl.BlockSpec(memory_space=pl.ANY)
    vmem = pltpu.VMEM

    def received(sub):
        return [vmem((3, 2, 24 * sub // 4**s, 128), f32) for s in range(3)]

    return pl.pallas_call(
        kernel,
        out_shape=jax.ShapeDtypeStruct((ROWS, COLS), bf16),
        in_specs=[any_space] * 3,
        out_specs=pl.BlockSpec(memory_space=vmem),
        scratch_shapes=[
            vmem((IN_PAIRS, 2 * LOCAL, PAIR), bf16),
            vmem((OUT_PAIRS, 2 * LOCAL, PAIR), bf16),
            vmem((ROWS, COLS), bf16),
            vmem((ROWS, COLS), bf16),
            vmem((ROWS, COLS), f32),
            vmem((3, 64 * SUB_IN, 128), f32),
            vmem((3, 64 * SUB_OUT, 128), f32),
            *received(SUB_IN),
            *received(SUB_OUT),
            vmem((3, 64, 128), f32),
            vmem((4, 3, 64, 128), bf16),
            vmem((8, 3, 64, 128), bf16),
            vmem((4, 256, 256), bf16),
            vmem((256, 256), bf16),
            vmem((256, 256), f32),
            vmem((2, 64, 128), f32),
            vmem((8, 128), f32),
            vmem((2, 8, 8, 128), f32),
            vmem((2, 16, 8, 128), f32),
            dma((IN_PAIRS,)),
            dma((OUT_PAIRS,)),
            dma((1,)),
            dma((IN_PAIRS,)),
            dma((1,)),
            dma((OUT_PAIRS,)),
            dma(()),
            dma((2, 3, 3)),
            dma((2, 3, 3, 6)),
            dma((7,)),
            dma((7,)),
            dma((8,)),
        ],
        compiler_params=pltpu.CompilerParams(
            collective_id=0, has_side_effects=True, vmem_limit_bytes=60 * 1024 * 1024
        ),
        name="kfac_step",
    )(tokens, grads, weight_grad)


def solution(mesh):
    every = P(("dp", "row", "col"), None)
    weight = P("row", ("dp", "col"))
    return jax.shard_map(
        on_device, mesh=mesh, in_specs=(every, every, weight), out_specs=weight, check_vma=False
    )
```

```python
import functools
import math

import jax
import jax.numpy as jnp
from jax import lax
from jax.experimental import pallas as pl
from jax.experimental.pallas import tpu as pltpu
from jax.sharding import PartitionSpec as P

D = 6144
F = 24576
BLOCK = 192
TOKENS = 32768
EPSILON = 1e-06
DAMP_ROOT = math.sqrt(0.01)
TRUST_RADIUS = 0.05

PAIR = 2 * BLOCK
LOCAL = 256
IN_PAIRS = 8
OUT_PAIRS = 32
DIRECT = ((0, 1), (0, 2), (1, 2))
AHEAD = 8
SUB_IN = 16
SUB_OUT = 64
ROWS = 768
COLS = 1536
MESH = pl.DeviceIdType.MESH
f32 = jnp.float32
bf16 = jnp.bfloat16


def mul(a, n):
    return pl.multiple_of(a, n)


def dot0(a, b):
    return lax.dot_general(a, b, (((0,), (0,)), ((), ())), preferred_element_type=f32)


def pair_pieces(data):
    turned = data.T
    d1 = jnp.dot(turned[0:256], data[:, 0:256], preferred_element_type=f32)
    d2 = jnp.dot(turned[128:384], data[:, 256:384], preferred_element_type=f32)
    low = lax.broadcasted_iota(jnp.int32, (64, 128), 1) < 64
    a = d1[0:128, 0:128]
    mid = d1[128:256, 128:256]
    b = d1[128:192, 0:128]
    even = (jnp.where(low, a[0:64], a[64:128]), jnp.where(low, mid[0:64], a[0:64]), b)
    a2 = d2[128:256]
    b2 = d2[64:128]
    odd = (jnp.where(low, a2[0:64], a2[64:128]), jnp.where(low, a2[64:128], mid[64:128]), b2)
    return even, odd


def pair_trace(even, odd):
    row = lax.broadcasted_iota(jnp.int32, (64, 128), 0)
    lane = lax.broadcasted_iota(jnp.int32, (64, 128), 1)
    first = lane == row
    second = lane == row + 64
    zero = jnp.zeros((64, 128), f32)
    total = jnp.where(first | second, even[0] + odd[0], zero)
    return total + jnp.where(first, even[1], zero) + jnp.where(second, odd[1], zero)


def frame(p0, p1, p2, parity, u_ref):
    low = lax.broadcasted_iota(jnp.int32, (64, 128), 1) < 64
    even = parity == 0
    zero = jnp.zeros((64, 128), f32)
    u_ref[0:64, 0:128] = jnp.where(even, jnp.where(low, p0, p1), zero)
    u_ref[0:64, 128:256] = zero
    u_ref[64:128, 0:128] = jnp.where(low, zero, jnp.where(even, p0, p1))
    u_ref[64:128, 128:256] = jnp.where(even, zero, p2)
    u_ref[128:192, 0:128] = jnp.where(even, p2, zero)
    u_ref[128:192, 128:256] = jnp.where(low, jnp.where(even, p1, p0), zero)
    u_ref[192:256, 0:128] = zero
    u_ref[192:256, 128:256] = jnp.where(even, zero, jnp.where(low, p1, p0))
    u = u_ref[...]
    row = lax.broadcasted_iota(jnp.int32, (256, 256), 0)
    col = lax.broadcasted_iota(jnp.int32, (256, 256), 1)
    same = lax.div(row, 64) == lax.div(col, 64)
    return u + jnp.where(same, 0.0, u.T)


def pack(own, off, even):
    def pick(a, b):
        return (a if even else b) if isinstance(even, bool) else jnp.where(even, a, b)

    low = lax.broadcasted_iota(jnp.int32, (64, 128), 1) < 64
    p0 = jnp.where(
        low,
        pick(own[0:64, 0:128], own[128:192, 128:256]),
        pick(own[64:128, 0:128], own[192:256, 128:256]),
    )
    p1 = jnp.where(
        low,
        pick(own[128:192, 128:256], off[192:256, 128:256]),
        pick(off[0:64, 0:128], own[64:128, 0:128]),
    )
    return p0, p1, pick(off[128:192, 0:128], off[64:128, 128:256])


def newton(p0, p1, p2, parity, shift, u_ref):
    even = parity == 0
    row = lax.broadcasted_iota(jnp.int32, (256, 256), 0)
    col = lax.broadcasted_iota(jnp.int32, (256, 256), 1)
    valid = jnp.where(even, (row < BLOCK).astype(f32), (row >= 64).astype(f32))
    eye = jnp.where(row == col, valid, 0.0)
    matrix = frame(p0, p1, p2, parity, u_ref) + shift * eye
    norm = jnp.sqrt(jnp.sum(jnp.sum(matrix * matrix, axis=1, keepdims=True), axis=0, keepdims=True))
    scale = 1.0 / norm
    dot = functools.partial(jnp.dot, precision=lax.Precision.HIGHEST, preferred_element_type=f32)
    r1 = eye - matrix * scale
    r2 = dot(r1, r1)
    r3 = dot(r1, r2)
    r4 = dot(r2, r2)
    low_sum = eye + r1 + r2 + r3
    inv = scale * (low_sum + dot(low_sum, r4))
    return [piece.astype(bf16) for piece in pack(inv, inv, even)]


def kernel(
    tok, grd, wgt, out,
    tbuf, gbuf, wbuf, left, nat, ai, ao,
    ri0, ri1, ri2, ro0, ro1, ro2,
    inp, ini, ino, invi, invo, tbl, u_ref, tr_acc, al_acc, ar1, ar2,
    tsem, gsem, tss, tsr, gss, gsr, wsem,
    nss, nsr, fss, fsr, gs, gr, orx,
):
    z = lax.axis_index("dp")
    row = lax.axis_index("row")
    col = lax.axis_index("col")
    xl = lax.div(row, 4)
    y = lax.rem(row, 4)
    xh = lax.div(col, 2)
    c = lax.rem(col, 2)
    x = xh * 2 + xl
    other = 1 - c
    pos = (x, y, z)

    def dev(xx, yy, zz, cc):
        return (zz, lax.rem(xx, 2) * 4 + yy, lax.div(xx, 2) * 2 + cc)

    def shifted(axis, delta):
        p = list(pos)
        p[axis] = lax.rem(p[axis] + delta, 4)
        return dev(*p, c)

    def remote(src, dst, ss, rs, device):
        pltpu.make_async_remote_copy(
            src_ref=src, dst_ref=dst, send_sem=ss, recv_sem=rs, device_id=device, device_id_type=MESH
        ).start()

    def wait(ref, sem):
        pltpu.make_async_copy(ref, ref, sem).wait()

    plane = []
    for j in range(1, 8):
        i = lax.rem(x * 2 + c + j, 8)
        plane.append(dev(lax.div(i, 2), y, z, lax.rem(i, 2)))
    sheet = []
    for j in range(1, 16):
        i = lax.rem(y * 4 + z + j, 16)
        sheet.append(dev(x, lax.div(i, 4), lax.rem(i, 4), c))
    diagonal = [dev(xh * 2 + 1 - xl, lax.rem(y + j, 4), z, c) for j in range(1, 4)]
    x_far, z_far = lax.rem(x + 2, 4), lax.rem(z + 2, 4)
    z_near = z + 1 - 2 * lax.rem(z, 2)
    corners = [dev(x_far, y, z, c), dev(x, y, z_far, c), dev(x_far, y, z_far, c)]
    cousins = [dev(x, y, z, other), dev(x, y, z_near, c), dev(x, y, z_near, other)]

    barrier = pltpu.get_barrier_semaphore()
    peers = plane + sheet + diagonal + [corners[2], cousins[2]]
    for device in peers:
        pl.semaphore_signal(barrier, inc=1, device_id=device, device_id_type=MESH)

    def tok_lanes(i, core):
        return pl.ds(mul((2 * i + core) * PAIR, 128), PAIR)

    def out_place(i):
        n = lax.div(i, 2)
        dx = lax.rem(2 + n, 4)
        dz = lax.rem(2 + n + lax.div(n, 4), 4)
        yh = lax.rem(lax.div(y, 2) + 1 + lax.rem(i, 2), 2)
        return lax.rem(x + dx, 4), yh, lax.rem(z + dz, 4)

    def grd_lanes(i, core):
        xx, yh, zz = out_place(i)
        pair = (zz * 4 + lax.div(xx, 2) * 2 + core) * 4 + lax.rem(xx, 2) * 2 + yh
        return pl.ds(mul(pair * PAIR, 128), PAIR)

    @pl.loop(0, IN_PAIRS)
    def _(i):
        pltpu.make_async_copy(tok.at[:, tok_lanes(i, c)], tbuf.at[i, 0:LOCAL], tsem.at[i]).start()

    @pl.loop(0, OUT_PAIRS)
    def _(i):
        pltpu.make_async_copy(grd.at[:, grd_lanes(i, c)], gbuf.at[i, 0:LOCAL], gsem.at[i]).start()

    pltpu.make_async_copy(wgt, wbuf, wsem).start()

    tr_acc[...] = jnp.zeros_like(tr_acc)
    nat[...] = jnp.zeros_like(nat)

    pl.semaphore_wait(barrier, len(peers))

    partner = dev(x, y, z, other)

    @pl.loop(0, IN_PAIRS)
    def _(i):
        remote(tok.at[:, tok_lanes(i, other)], tbuf.at[i, LOCAL:], tss.at[0], tsr.at[i], partner)

    def swap_out(i):
        remote(grd.at[:, grd_lanes(i, other)], gbuf.at[i, LOCAL:], gss.at[0], gsr.at[i], partner)

    @pl.loop(0, AHEAD)
    def _(i):
        swap_out(i)

    def index(p, xx, yy, zz):
        t = (xx, yy, zz)
        return t[p] * 16 + t[(p + 1) % 3] * 4 + t[(p + 2) % 3]

    def base(p, stage, sub):
        b = 0
        for s in range(stage):
            b = b + pos[(p + s) % 3] * ((16, 4, 1)[s] * sub)
        return b

    class Ring:
        def __init__(self, axis, buf, recv, ss, rs, b, stride, n):
            self.axis, self.buf, self.recv, self.ss, self.rs = axis, buf, recv, ss, rs
            self.b, self.stride, self.n, self.h = b, stride, n, n // 2

        def part(self, step, offset, rows):
            return pl.ds(mul(self.b + lax.rem(pos[self.axis] + step, 4) * self.stride + offset, 8), rows)

        def place(self, direction, kind, offset):
            return self.recv.at[direction, pl.ds(0 if kind == 0 else self.h + offset, self.h)]

        def send(self, direction, kind, step, offset):
            remote(
                self.buf.at[self.part(step, offset, self.h)], self.place(direction, kind, offset),
                self.ss, self.rs.at[2 * kind + direction], shifted(self.axis, 3 if direction else 1),
            )

        def got(self, direction, kind, offset):
            wait(self.place(direction, kind, offset), self.rs.at[2 * kind + direction])

        def far(self):
            self.send(0, 0, 2, 0)
            self.send(1, 0, 2, self.h)

        def near(self, direction):
            self.send(direction, 1, 3 if direction else 1, 0 if direction else self.h)

        def issue(self):
            self.far()
            self.near(0)
            self.near(1)

        def relay_one(self, direction):
            step, offset = (3, self.h) if direction else (1, 0)
            self.got(direction, 0, 0)
            rows = self.part(step, offset, self.h)
            self.buf[rows] = self.buf[rows] + self.recv[direction, 0 : self.h]
            self.send(direction, 2, step, offset)

        def relay(self):
            self.relay_one(0)
            self.relay_one(1)

        def final(self):
            h, n = self.h, self.n
            self.got(0, 1, h)
            self.got(1, 1, 0)
            self.got(0, 2, 0)
            self.got(1, 2, h)
            rows = self.part(0, 0, n)
            self.buf[rows] = self.buf[rows] + self.recv[0, h : h + n] + self.recv[1, h : h + n]

    class Direct(Ring):
        def issue(self):
            n = self.n
            for k in (2, 1, 3):
                remote(
                    self.buf.at[self.part(k, 0, n)], self.recv.at[k - 1], self.ss, self.rs.at[k - 1],
                    shifted(self.axis, k),
                )

        def final(self):
            for k in (1, 3, 2):
                wait(self.recv.at[k - 1], self.rs.at[k - 1])
            rows = self.part(0, 0, self.n)
            self.buf[rows] = self.buf[rows] + self.recv[0] + self.recv[1] + self.recv[2]

    def whole_ring(net, stage, p):
        sub = (SUB_IN, SUB_OUT)[net]
        n = (16, 4, 1)[stage] * sub
        recv = ((ri0, ri1, ri2), (None, ro1, ro2))[net][stage]
        kind = Direct if (net, stage) in DIRECT else Ring
        return kind(
            (p + stage) % 3, (ai, ao)[net].at[p], recv.at[p], nss.at[net, stage, p], nsr.at[net, stage, p],
            base(p, stage, sub), n, n,
        )

    def first_ring(p, step):
        second = lax.rem(pos[(p + 1) % 3] + step, 4)
        return Ring(
            p, ao.at[p], ro0.at[p, second], fss.at[p, second], fsr.at[p, second],
            second * 4 * SUB_OUT, 16 * SUB_OUT, 4 * SUB_OUT,
        )

    @pl.loop(0, IN_PAIRS)
    def _(i):
        swap_out(AHEAD + i)
        wait(tbuf.at[i, 0:LOCAL], tsem.at[i])
        wait(tbuf.at[i, LOCAL:], tsr.at[i])
        pieces = pair_pieces(tbuf[i])
        tr_acc[1] = tr_acc[1] + pair_trace(*pieces)
        for e in range(2):
            for p in range(3):
                for q in range(4):
                    xx = q // 2 * 2 + lax.div(i, 4)
                    at = index(p, xx, lax.rem(i, 4), q % 2 * 2 + e) * SUB_IN
                    ai[p, pl.ds(mul(at, SUB_IN), SUB_IN)] = pieces[e][p][q * 16 : q * 16 + 16]

    in_rings = [[whole_ring(0, s, p) for p in range(3)] for s in range(3)]
    out_rings = [None] + [[whole_ring(1, s, p) for p in range(3)] for s in range(1, 3)]
    for p in range(3):
        in_rings[0][p].issue()

    order = (2, 0, 1)

    def advance(rings, stage):
        for p in order:
            rings[stage][p].final()
            rings[stage + 1][p].issue()

    @pl.loop(0, OUT_PAIRS)
    def _(i):
        @pl.when(i == 14)
        def _():
            for p in order:
                in_rings[0][p].relay()

        @pl.when(i == 28)
        def _():
            advance(in_rings, 0)

        @pl.when(i < OUT_PAIRS - AHEAD - IN_PAIRS)
        def _():
            swap_out(AHEAD + IN_PAIRS + i)

        xx, yh, zz = out_place(i)
        wait(gbuf.at[i, 0:LOCAL], gsem.at[i])
        wait(gbuf.at[i, LOCAL:], gsr.at[i])
        pieces = pair_pieces(gbuf[i])
        tr_acc[0] = tr_acc[0] + pair_trace(*pieces)
        for p, e in ((2, 0), (2, 1), (0, 0), (0, 1), (1, 0), (1, 1)):
            place = (xx, 2 * yh + e, zz)
            second, third = place[(p + 1) % 3], place[(p + 2) % 3]
            at = mul((place[p] * 16 + second * 4 + third) * SUB_OUT, SUB_OUT)
            ao[p, pl.ds(at, SUB_OUT)] = pieces[e][p]
            if p == 2 and e == 0:
                continue
            count = SUB_OUT
            if p == 2:
                count, third, at = 2 * SUB_OUT, 2 * yh, mul(at - SUB_OUT, SUB_OUT)
            d = lax.rem(place[p] - pos[p] + 4, 4)
            h = lax.div(third, 2)
            far = (1 - lax.rem(d, 2)) * lax.div(d, 2)
            go = far + lax.rem(d, 2) * lax.rem(lax.div(d, 2) + h, 2)
            direction = far * h + (1 - far) * (1 - h)
            to = (far * lax.rem(third, 2) + (1 - far) * (2 + third)) * SUB_OUT

            @pl.when(go == 1)
            def _():
                remote(
                    ao.at[p, pl.ds(at, count)],
                    ro0.at[p, second, direction, pl.ds(mul(to, SUB_OUT), count)],
                    fss.at[p, second], fsr.at[p, second, 2 * (1 - far) + direction],
                    shifted(p, 1 + 2 * direction),
                )

    def reduce_start(use, value):
        mine = x * 2 + c
        ar1[use, mine] = value
        for device in plane:
            remote(ar1.at[use, mine], ar1.at[use, mine], gs.at[use], gr.at[use], device)

    def reduce_middle(use):
        wait(ar1.at[use, 0:7], gr.at[use])
        mine = y * 4 + z
        ar2[use, mine] = jnp.sum(ar1[use], axis=0)
        for device in sheet:
            remote(ar2.at[use, mine], ar2.at[use, mine], gs.at[2 + use], gr.at[2 + use], device)

    def reduce_end(use):
        wait(ar2.at[use, 0:15], gr.at[2 + use])
        return jnp.sum(ar2[use], axis=0)

    def total(value):
        return jnp.sum(jnp.sum(value, axis=1, keepdims=True), axis=0, keepdims=True)

    t_out = jnp.sum(tr_acc[0].reshape(16, 4, 128), axis=0)
    t_in = jnp.sum(tr_acc[1].reshape(16, 4, 128), axis=0)
    reduce_start(0, jnp.concatenate([t_out, t_in], axis=0))

    for p in order:
        first_ring(p, 2).relay()
    for t in (1, 3):
        for p in order:
            first_ring(p, t).relay()
    reduce_middle(0)
    for p in order:
        first_ring(p, 2).final()
        out_rings[1][p].far()
    advance(in_rings, 1)
    for p in order:
        first_ring(p, 0).relay()
    for p in order:
        first_ring(p, 1).final()
        out_rings[1][p].near(0)
    for p in order:
        first_ring(p, 3).final()
        out_rings[1][p].near(1)
    for p in order:
        out_rings[1][p].relay()
    for p in order:
        in_rings[2][p].final()

    quarter = pl.ds(mul((xh * 2 + lax.div(z, 2)) * SUB_IN, SUB_IN), SUB_IN)
    for p in range(3):
        inp[p, quarter] = ai[p, pl.ds(mul(index(p, x, y, z) * SUB_IN, SUB_IN), SUB_IN)]
    for device in corners:
        remote(inp.at[:, quarter], inp.at[:, quarter], gs.at[4], gr.at[4], device)

    traces = reduce_end(0)
    inverse_count = 1.0 / TOKENS
    trace_out = total(traces[0:4]) * inverse_count
    trace_in = total(traces[4:8]) * inverse_count
    ratio = jnp.sqrt((trace_in / D + EPSILON) / (trace_out / F + EPSILON))
    for p in order:
        first_ring(p, 0).final()
    advance(out_rings, 1)
    wait(inp.at[:, 0:48], gr.at[4])
    slot = c * 2 + lax.rem(z, 2)
    mine = [inp[p] * inverse_count for p in range(3)]
    for p, piece in enumerate(newton(*mine, lax.rem(z, 2), ratio * DAMP_ROOT, u_ref)):
        ini[slot, p] = piece
    for device in cousins:
        remote(ini.at[slot], ini.at[slot], gs.at[5], gr.at[5], device)

    for p in order:
        out_rings[2][p].final()

    own = [
        ao[p, pl.ds(mul(index(p, x, y, z) * SUB_OUT, SUB_OUT), SUB_OUT)] * inverse_count for p in range(3)
    ]
    for p, piece in enumerate(newton(*own, lax.rem(y, 2), DAMP_ROOT / ratio, u_ref)):
        ino[row, p] = piece
    for j in range(1, 8):
        i = lax.rem(row + j, 8)
        remote(ino.at[row], ino.at[row], gs.at[6], orx.at[row], (z, i, col))
    al_acc[...] = jnp.zeros_like(al_acc)

    wait(wbuf, wsem)
    wait(ini.at[0:3], gr.at[5])

    @pl.loop(0, 4)
    def _(k):
        pieces = [ini[k, p].astype(f32) for p in range(3)]
        invi[k] = frame(*pieces, lax.rem(k, 2), u_ref).astype(bf16)

    @pl.loop(0, 4)
    def _(n):
        lanes = pl.ds(mul(n * PAIR, 128), PAIR)
        for q in range(2):
            at = q * PAIR
            first = jnp.dot(
                invi[2 * q, 0:192], wbuf[at : at + 256, lanes], preferred_element_type=f32
            )
            second = jnp.dot(
                invi[2 * q + 1, 64:256], wbuf[at + 128 : at + 384, lanes], preferred_element_type=f32
            )
            left[at : at + 192, lanes] = first.astype(bf16)
            left[at + 192 : at + 384, lanes] = second.astype(bf16)

    @pl.loop(0, 4)
    def _(q):
        for e in range(2):
            lanes = pl.ds(mul(q * PAIR + e * 128, 128), 256)
            grown = dot0(left[:, lanes], wbuf[:, lanes])
            for p, piece in enumerate(pack(grown, grown + grown.T, e == 0)):
                tbl[2 * q + e, p] = piece

    def arrival(j):
        m = lax.rem(j, 4)
        yy = lax.rem(y + m + lax.div(m, 2) * (5 - 2 * m), 4)
        return lax.rem(xl + lax.div(j, 4), 2) * 4 + yy

    @pl.loop(0, 8)
    def _(j):
        k = arrival(j)

        @pl.when(j > 0)
        def _():
            wait(ino.at[k], orx.at[k])

        product = tbl[k] * ino[k].astype(f32)
        al_acc[...] = al_acc[...] + jnp.sum(product.reshape(24, 8, 128), axis=0)

    reduce_start(1, al_acc[...])

    @pl.loop(0, 8)
    def _(k):
        @pl.when(k == 6)
        def _():
            reduce_middle(1)

        pieces = [ino[k, p].astype(f32) for p in range(3)]
        invo[...] = frame(*pieces, lax.rem(k, 2), u_ref).astype(bf16)
        lanes = pl.ds(mul(lax.div(k, 2) * PAIR + lax.rem(k, 2) * 128, 128), 256)
        for n in range(3):
            rows = pl.ds(n * 256, 256)
            part = jnp.dot(left[rows, lanes], invo[...], preferred_element_type=f32)
            nat[rows, lanes] = nat[rows, lanes] + part

    alignment = total(reduce_end(1))
    factor = jnp.sqrt(TRUST_RADIUS * D * F / alignment)
    out[...] = (nat[...] * factor).astype(bf16)

    wait(tbuf.at[:, LOCAL:], tss.at[0])
    wait(gbuf.at[:, LOCAL:], gss.at[0])
    for p in range(3):
        for t in range(4):
            wait(ro0.at[p, t], fss.at[p, t])
        for net, s, recv in ((0, 0, ri0), (0, 1, ri1), (0, 2, ri2), (1, 1, ro1), (1, 2, ro2)):
            wait(recv.at[p], nss.at[net, s, p])
    for use in range(2):
        wait(ar1.at[use, 0:7], gs.at[use])
        wait(ar2.at[use, 0:15], gs.at[2 + use])
    wait(inp.at[:, 0:48], gs.at[4])
    wait(ini.at[0:3], gs.at[5])
    wait(ino.at[0:7], gs.at[6])


def on_device(tokens, grads, weight_grad):
    dma = pltpu.SemaphoreType.DMA
    any_space = pl.BlockSpec(memory_space=pltpu.HBM)
    vmem = pltpu.VMEM

    def received(net, sub):
        sizes = [24 * sub // 4**s for s in range(3)]
        return [
            vmem((3, 3, n * 2 // 3, 128) if (net, s) in DIRECT else (3, 2, n, 128), f32)
            for s, n in enumerate(sizes)
        ]

    return pl.pallas_call(
        kernel,
        out_shape=jax.ShapeDtypeStruct((ROWS, COLS), bf16),
        in_specs=[any_space] * 3,
        out_specs=pl.BlockSpec(memory_space=vmem),
        scratch_shapes=[
            vmem((IN_PAIRS, 2 * LOCAL, PAIR), bf16),
            vmem((OUT_PAIRS, 2 * LOCAL, PAIR), bf16),
            vmem((ROWS, COLS), bf16),
            vmem((ROWS, COLS), bf16),
            vmem((ROWS, COLS), f32),
            vmem((3, 64 * SUB_IN, 128), f32),
            vmem((3, 64 * SUB_OUT, 128), f32),
            *received(0, SUB_IN),
            vmem((3, 4, 2, 6 * SUB_OUT, 128), f32),
            *received(1, SUB_OUT)[1:],
            vmem((3, 64, 128), f32),
            vmem((4, 3, 64, 128), bf16),
            vmem((8, 3, 64, 128), bf16),
            vmem((4, 256, 256), bf16),
            vmem((256, 256), bf16),
            vmem((8, 3, 64, 128), f32),
            vmem((256, 256), f32),
            vmem((2, 64, 128), f32),
            vmem((8, 128), f32),
            vmem((2, 8, 8, 128), f32),
            vmem((2, 16, 8, 128), f32),
            dma((IN_PAIRS,)),
            dma((OUT_PAIRS,)),
            dma((1,)),
            dma((IN_PAIRS,)),
            dma((1,)),
            dma((OUT_PAIRS,)),
            dma(()),
            dma((2, 3, 3)),
            dma((2, 3, 3, 6)),
            dma((3, 4)),
            dma((3, 4, 6)),
            dma((7,)),
            dma((7,)),
            dma((8,)),
        ],
        compiler_params=pltpu.CompilerParams(
            collective_id=0, has_side_effects=True, vmem_limit_bytes=50 * 1024 * 1024
        ),
        name="kfac_step",
    )(tokens, grads, weight_grad)


def solution(mesh):
    every = P(("dp", "row", "col"), None)
    weight = P("row", ("dp", "col"))
    return jax.shard_map(
        on_device, mesh=mesh, in_specs=(every, every, weight), out_specs=weight, check_vma=False
    )
```

```python
import functools
import math

import jax
import jax.numpy as jnp
from jax import lax
from jax.experimental import pallas as pl
from jax.experimental.pallas import tpu as pltpu
from jax.sharding import PartitionSpec as P

D = 6144
F = 24576
BLOCK = 192
TOKENS = 32768
EPSILON = 1e-06
DAMP_ROOT = math.sqrt(0.01)
TRUST_RADIUS = 0.05

PAIR = 2 * BLOCK
LOCAL = 256
IN_PAIRS = 8
OUT_PAIRS = 32
DIRECT = ((0, 1), (0, 2), (1, 2))
STEPS_AT = (7, 14)
AHEAD = 8
SUB_IN = 16
SUB_OUT = 64
ROWS = 768
COLS = 1536
MESH = pl.DeviceIdType.MESH
f32 = jnp.float32
bf16 = jnp.bfloat16


def mul(a, n):
    return pl.multiple_of(a, n)


def dot0(a, b):
    return lax.dot_general(a, b, (((0,), (0,)), ((), ())), preferred_element_type=f32)


def pair_pieces(data):
    turned = data.T
    d1 = jnp.dot(turned[0:256], data[:, 0:256], preferred_element_type=f32)
    d2 = jnp.dot(turned[128:384], data[:, 256:384], preferred_element_type=f32)
    low = lax.broadcasted_iota(jnp.int32, (64, 128), 1) < 64
    a = d1[0:128, 0:128]
    mid = d1[128:256, 128:256]
    b = d1[128:192, 0:128]
    even = (jnp.where(low, a[0:64], a[64:128]), jnp.where(low, mid[0:64], a[0:64]), b)
    a2 = d2[128:256]
    b2 = d2[64:128]
    odd = (jnp.where(low, a2[0:64], a2[64:128]), jnp.where(low, a2[64:128], mid[64:128]), b2)
    return even, odd


def pair_trace(even, odd):
    row = lax.broadcasted_iota(jnp.int32, (64, 128), 0)
    lane = lax.broadcasted_iota(jnp.int32, (64, 128), 1)
    first = lane == row
    second = lane == row + 64
    zero = jnp.zeros((64, 128), f32)
    total = jnp.where(first | second, even[0] + odd[0], zero)
    return total + jnp.where(first, even[1], zero) + jnp.where(second, odd[1], zero)


def frame(p0, p1, p2, parity, u_ref):
    low = lax.broadcasted_iota(jnp.int32, (64, 128), 1) < 64
    even = parity == 0
    zero = jnp.zeros((64, 128), f32)
    u_ref[0:64, 0:128] = jnp.where(even, jnp.where(low, p0, p1), zero)
    u_ref[0:64, 128:256] = zero
    u_ref[64:128, 0:128] = jnp.where(low, zero, jnp.where(even, p0, p1))
    u_ref[64:128, 128:256] = jnp.where(even, zero, p2)
    u_ref[128:192, 0:128] = jnp.where(even, p2, zero)
    u_ref[128:192, 128:256] = jnp.where(low, jnp.where(even, p1, p0), zero)
    u_ref[192:256, 0:128] = zero
    u_ref[192:256, 128:256] = jnp.where(even, zero, jnp.where(low, p1, p0))
    u = u_ref[...]
    row = lax.broadcasted_iota(jnp.int32, (256, 256), 0)
    col = lax.broadcasted_iota(jnp.int32, (256, 256), 1)
    same = lax.div(row, 64) == lax.div(col, 64)
    return u + jnp.where(same, 0.0, u.T)


def pack(own, off, even):
    def pick(a, b):
        return (a if even else b) if isinstance(even, bool) else jnp.where(even, a, b)

    low = lax.broadcasted_iota(jnp.int32, (64, 128), 1) < 64
    p0 = jnp.where(
        low,
        pick(own[0:64, 0:128], own[128:192, 128:256]),
        pick(own[64:128, 0:128], own[192:256, 128:256]),
    )
    p1 = jnp.where(
        low,
        pick(own[128:192, 128:256], off[192:256, 128:256]),
        pick(off[0:64, 0:128], own[64:128, 0:128]),
    )
    return p0, p1, pick(off[128:192, 0:128], off[64:128, 128:256])


def newton(p0, p1, p2, parity, shift, u_ref):
    even = parity == 0
    row = lax.broadcasted_iota(jnp.int32, (256, 256), 0)
    col = lax.broadcasted_iota(jnp.int32, (256, 256), 1)
    valid = jnp.where(even, (row < BLOCK).astype(f32), (row >= 64).astype(f32))
    eye = jnp.where(row == col, valid, 0.0)
    matrix = frame(p0, p1, p2, parity, u_ref) + shift * eye
    norm = jnp.sqrt(jnp.sum(jnp.sum(matrix * matrix, axis=1, keepdims=True), axis=0, keepdims=True))
    scale = 1.0 / norm
    dot = functools.partial(jnp.dot, precision=lax.Precision.HIGHEST, preferred_element_type=f32)
    r1 = eye - matrix * scale
    r2 = dot(r1, r1)
    r3 = dot(r1, r2)
    r4 = dot(r2, r2)
    low_sum = eye + r1 + r2 + r3
    inv = scale * (low_sum + dot(low_sum, r4))
    return [piece.astype(bf16) for piece in pack(inv, inv, even)]


def kernel(
    tok, grd, wgt, out,
    tbuf, gbuf, wbuf, left, nat, ai, ao,
    ri0, ri1, ri2, ro0, ro1, ro2,
    inp, ini, ino, invi, invo, tbl, u_ref, tr_acc, al_acc, ar1, ar2,
    tsem, gsem, tss, gss, wsem,
    nss, nsr, fss, fsr, gs, gr, orx,
):
    z = lax.axis_index("dp")
    row = lax.axis_index("row")
    col = lax.axis_index("col")
    xl = lax.div(row, 4)
    y = lax.rem(row, 4)
    xh = lax.div(col, 2)
    c = lax.rem(col, 2)
    x = xh * 2 + xl
    other = 1 - c
    pos = (x, y, z)

    def dev(xx, yy, zz, cc):
        return (zz, lax.rem(xx, 2) * 4 + yy, lax.div(xx, 2) * 2 + cc)

    def shifted(axis, delta):
        p = list(pos)
        p[axis] = lax.rem(p[axis] + delta, 4)
        return dev(*p, c)

    def remote(src, dst, ss, rs, device):
        pltpu.make_async_remote_copy(
            src_ref=src, dst_ref=dst, send_sem=ss, recv_sem=rs, device_id=device, device_id_type=MESH
        ).start()

    def wait(ref, sem):
        pltpu.make_async_copy(ref, ref, sem).wait()

    plane = []
    for j in range(1, 8):
        i = lax.rem(x * 2 + c + j, 8)
        plane.append(dev(lax.div(i, 2), y, z, lax.rem(i, 2)))
    sheet = []
    for j in range(1, 16):
        i = lax.rem(y * 4 + z + j, 16)
        sheet.append(dev(x, lax.div(i, 4), lax.rem(i, 4), c))
    diagonal = [dev(xh * 2 + 1 - xl, lax.rem(y + j, 4), z, c) for j in range(1, 4)]
    x_far, z_far = lax.rem(x + 2, 4), lax.rem(z + 2, 4)
    z_near = z + 1 - 2 * lax.rem(z, 2)
    corners = [dev(x_far, y, z, c), dev(x, y, z_far, c), dev(x_far, y, z_far, c)]
    cousins = [dev(x, y, z, other), dev(x, y, z_near, c), dev(x, y, z_near, other)]

    barrier = pltpu.get_barrier_semaphore()
    peers = plane + sheet + diagonal + [corners[2], cousins[2]]
    for device in peers:
        pl.semaphore_signal(barrier, inc=1, device_id=device, device_id_type=MESH)

    def tok_lanes(i, core):
        return pl.ds(mul((2 * i + core) * PAIR, 128), PAIR)

    def out_place(i):
        n = lax.div(i, 2)
        dx = lax.rem(2 + n, 4)
        dz = lax.rem(2 + n + lax.div(n, 4), 4)
        yh = lax.rem(lax.div(y, 2) + 1 + lax.rem(i, 2), 2)
        return lax.rem(x + dx, 4), yh, lax.rem(z + dz, 4)

    def grd_lanes(i, core):
        xx, yh, zz = out_place(i)
        pair = (zz * 4 + lax.div(xx, 2) * 2 + core) * 4 + lax.rem(xx, 2) * 2 + yh
        return pl.ds(mul(pair * PAIR, 128), PAIR)

    @pl.loop(0, IN_PAIRS)
    def _(i):
        pltpu.make_async_copy(tok.at[:, tok_lanes(i, c)], tbuf.at[i, 0:LOCAL], tsem.at[lax.div(i, 2)]).start()

    @pl.loop(0, OUT_PAIRS)
    def _(i):
        pltpu.make_async_copy(grd.at[:, grd_lanes(i, c)], gbuf.at[i, 0:LOCAL], gsem.at[lax.div(i, 2)]).start()

    pltpu.make_async_copy(wgt, wbuf, wsem).start()

    tr_acc[...] = jnp.zeros_like(tr_acc)
    nat[...] = jnp.zeros_like(nat)

    pl.semaphore_wait(barrier, len(peers))

    partner = dev(x, y, z, other)

    @pl.loop(0, IN_PAIRS)
    def _(i):
        remote(tok.at[:, tok_lanes(i, other)], tbuf.at[i, LOCAL:], tss.at[0], tsem.at[lax.div(i, 2)], partner)

    def swap_out(i):
        remote(grd.at[:, grd_lanes(i, other)], gbuf.at[i, LOCAL:], gss.at[0], gsem.at[lax.div(i, 2)], partner)

    @pl.loop(0, AHEAD)
    def _(i):
        swap_out(i)

    def index(p, xx, yy, zz):
        t = (xx, yy, zz)
        return t[p] * 16 + t[(p + 1) % 3] * 4 + t[(p + 2) % 3]

    def base(p, stage, sub):
        b = 0
        for s in range(stage):
            b = b + pos[(p + s) % 3] * ((16, 4, 1)[s] * sub)
        return b

    class Ring:
        def __init__(self, axis, buf, recv, ss, rs, b, stride, n):
            self.axis, self.buf, self.recv, self.ss, self.rs = axis, buf, recv, ss, rs
            self.b, self.stride, self.n, self.h = b, stride, n, n // 2

        def part(self, step, offset, rows):
            return pl.ds(mul(self.b + lax.rem(pos[self.axis] + step, 4) * self.stride + offset, 8), rows)

        def place(self, direction, kind, offset):
            return self.recv.at[direction, pl.ds(0 if kind == 0 else self.h + offset, self.h)]

        def send(self, direction, kind, step, offset):
            remote(
                self.buf.at[self.part(step, offset, self.h)], self.place(direction, kind, offset),
                self.ss, self.rs[min(kind, 1)], shifted(self.axis, 3 if direction else 1),
            )

        def far(self):
            self.send(0, 0, 2, 0)
            self.send(1, 0, 2, self.h)

        def near(self, direction):
            self.send(direction, 1, 3 if direction else 1, 0 if direction else self.h)

        def issue(self):
            self.far()
            self.near(0)
            self.near(1)

        def relay(self):
            wait(self.recv.at[:, pl.ds(0, self.h)], self.rs[0])
            for direction, step, offset in ((0, 1, 0), (1, 3, self.h)):
                rows = self.part(step, offset, self.h)
                self.buf[rows] = self.buf[rows] + self.recv[direction, 0 : self.h]
                self.send(direction, 2, step, offset)

        def final(self):
            h, n = self.h, self.n
            wait(self.recv.at[:, pl.ds(h, n)], self.rs[1])
            rows = self.part(0, 0, n)
            self.buf[rows] = self.buf[rows] + self.recv[0, h : h + n] + self.recv[1, h : h + n]

    class Direct(Ring):
        def issue(self):
            n = self.n
            for k in (2, 1, 3):
                remote(
                    self.buf.at[self.part(k, 0, n)], self.recv.at[k - 1], self.ss, self.rs[0],
                    shifted(self.axis, k),
                )

        def final(self):
            wait(self.recv, self.rs[0])
            rows = self.part(0, 0, self.n)
            self.buf[rows] = self.buf[rows] + self.recv[0] + self.recv[1] + self.recv[2]

    def whole_ring(net, stage, p):
        sub = (SUB_IN, SUB_OUT)[net]
        n = (16, 4, 1)[stage] * sub
        recv = ((ri0, ri1, ri2), (None, ro1, ro2))[net][stage]
        kind = Direct if (net, stage) in DIRECT else Ring
        place = {(0, 0): 0, (1, 1): 2, (0, 1): 4, (0, 2): 5, (1, 2): 6}[net, stage]
        return kind(
            (p + stage) % 3, (ai, ao)[net].at[p], recv.at[p], nss.at[3 * net + stage], [nsr.at[p, place + k] for k in range(1 if kind is Direct else 2)],
            base(p, stage, sub), n, n,
        )

    def first_ring(p, step):
        second = lax.rem(pos[(p + 1) % 3] + step, 4)
        return Ring(
            p, ao.at[p], ro0.at[p, second], fss.at[0], [fsr.at[p, second, 0], fsr.at[p, second, 1]],
            second * 4 * SUB_OUT, 16 * SUB_OUT, 4 * SUB_OUT,
        )

    @pl.loop(0, IN_PAIRS // 2)
    def _(n):
        for u in range(2):
            swap_out(AHEAD + 2 * n + u)
        done = []
        wait(tbuf.at[pl.ds(2 * n, 2)], tsem.at[n])
        for u in range(2):
            done.append(pair_pieces(tbuf[2 * n + u]))
        tr_acc[1] = tr_acc[1] + (pair_trace(*done[0]) + pair_trace(*done[1]))
        for u, pieces in enumerate(done):
            i = 2 * n + u
            for e in range(2):
                for p in range(3):
                    for q in range(4):
                        xx = q // 2 * 2 + lax.div(i, 4)
                        at = index(p, xx, lax.rem(i, 4), q % 2 * 2 + e) * SUB_IN
                        ai[p, pl.ds(mul(at, SUB_IN), SUB_IN)] = pieces[e][p][q * 16 : q * 16 + 16]

    in_rings = [[whole_ring(0, s, p) for p in range(3)] for s in range(3)]
    out_rings = [None] + [[whole_ring(1, s, p) for p in range(3)] for s in range(1, 3)]
    for p in range(3):
        in_rings[0][p].issue()

    order = (2, 0, 1)

    def advance(rings, stage):
        for p in order:
            rings[stage][p].final()
            rings[stage + 1][p].issue()

    @pl.loop(0, OUT_PAIRS // 2)
    def _(n):
        @pl.when(n == STEPS_AT[0])
        def _():
            for p in order:
                in_rings[0][p].relay()

        @pl.when(n == STEPS_AT[1])
        def _():
            advance(in_rings, 0)

        @pl.when(n < (OUT_PAIRS - AHEAD - IN_PAIRS) // 2)
        def _():
            for u in range(2):
                swap_out(AHEAD + IN_PAIRS + 2 * n + u)

        wait(gbuf.at[pl.ds(2 * n, 2)], gsem.at[n])
        done = [pair_pieces(gbuf[2 * n + u]) for u in range(2)]
        tr_acc[0] = tr_acc[0] + (pair_trace(*done[0]) + pair_trace(*done[1]))
        sends = []
        for u, pieces in enumerate(done):
            xx, yh, zz = out_place(2 * n + u)
            for p, e in ((2, 0), (2, 1), (0, 0), (0, 1), (1, 0), (1, 1)):
                place = (xx, 2 * yh + e, zz)
                second, third = place[(p + 1) % 3], place[(p + 2) % 3]
                at = mul((place[p] * 16 + second * 4 + third) * SUB_OUT, SUB_OUT)
                ao[p, pl.ds(at, SUB_OUT)] = pieces[e][p]
                if p < 2:
                    sends.append((p, place[p], second, third, at, SUB_OUT))
                elif e == 0:
                    sends.append((p, place[p], second, third, at, 2 * SUB_OUT))
        for p, first, second, third, at, count in sends:
            d = lax.rem(first - pos[p] + 4, 4)
            h = lax.div(third, 2)
            far = (1 - lax.rem(d, 2)) * lax.div(d, 2)
            go = far + lax.rem(d, 2) * lax.rem(lax.div(d, 2) + h, 2)
            direction = far * h + (1 - far) * (1 - h)
            to = (far * lax.rem(third, 2) + (1 - far) * (2 + third)) * SUB_OUT

            @pl.when(go == 1)
            def _():
                remote(
                    ao.at[p, pl.ds(at, count)],
                    ro0.at[p, second, direction, pl.ds(mul(to, SUB_OUT), count)],
                    fss.at[0], fsr.at[p, second, 1 - far],
                    shifted(p, 1 + 2 * direction),
                )

    def reduce_start(use, value):
        mine = x * 2 + c
        ar1[use, mine] = value
        for device in plane:
            remote(ar1.at[use, mine], ar1.at[use, mine], gs.at[use], gr.at[use], device)

    def reduce_middle(use):
        wait(ar1.at[use, 0:7], gr.at[use])
        mine = y * 4 + z
        ar2[use, mine] = jnp.sum(ar1[use], axis=0)
        for device in sheet:
            remote(ar2.at[use, mine], ar2.at[use, mine], gs.at[2 + use], gr.at[2 + use], device)

    def reduce_end(use):
        wait(ar2.at[use, 0:15], gr.at[2 + use])
        return jnp.sum(ar2[use], axis=0)

    def total(value):
        return jnp.sum(jnp.sum(value, axis=1, keepdims=True), axis=0, keepdims=True)

    t_out = jnp.sum(tr_acc[0].reshape(16, 4, 128), axis=0)
    t_in = jnp.sum(tr_acc[1].reshape(16, 4, 128), axis=0)
    reduce_start(0, jnp.concatenate([t_out, t_in], axis=0))

    for p in order:
        first_ring(p, 2).relay()
    for t in (1, 3):
        for p in order:
            first_ring(p, t).relay()
    reduce_middle(0)
    for p in order:
        first_ring(p, 2).final()
        out_rings[1][p].far()
    advance(in_rings, 1)
    for p in order:
        first_ring(p, 0).relay()
    for p in order:
        first_ring(p, 1).final()
        out_rings[1][p].near(0)
    for p in order:
        first_ring(p, 3).final()
        out_rings[1][p].near(1)
    for p in order:
        out_rings[1][p].relay()
    for p in order:
        in_rings[2][p].final()

    quarter = pl.ds(mul((xh * 2 + lax.div(z, 2)) * SUB_IN, SUB_IN), SUB_IN)
    for p in range(3):
        inp[p, quarter] = ai[p, pl.ds(mul(index(p, x, y, z) * SUB_IN, SUB_IN), SUB_IN)]
    for device in corners:
        remote(inp.at[:, quarter], inp.at[:, quarter], gs.at[4], gr.at[4], device)

    traces = reduce_end(0)
    inverse_count = 1.0 / TOKENS
    trace_out = total(traces[0:4]) * inverse_count
    trace_in = total(traces[4:8]) * inverse_count
    ratio = jnp.sqrt((trace_in / D + EPSILON) / (trace_out / F + EPSILON))
    for p in order:
        first_ring(p, 0).final()
    advance(out_rings, 1)
    wait(inp.at[:, 0:48], gr.at[4])
    slot = c * 2 + lax.rem(z, 2)
    mine = [inp[p] * inverse_count for p in range(3)]
    for p, piece in enumerate(newton(*mine, lax.rem(z, 2), ratio * DAMP_ROOT, u_ref)):
        ini[slot, p] = piece
    for device in cousins:
        remote(ini.at[slot], ini.at[slot], gs.at[5], gr.at[5], device)

    for p in order:
        out_rings[2][p].final()

    own = [
        ao[p, pl.ds(mul(index(p, x, y, z) * SUB_OUT, SUB_OUT), SUB_OUT)] * inverse_count for p in range(3)
    ]
    for p, piece in enumerate(newton(*own, lax.rem(y, 2), DAMP_ROOT / ratio, u_ref)):
        ino[row, p] = piece
    for j in range(1, 8):
        i = lax.rem(row + j, 8)
        remote(ino.at[row], ino.at[row], gs.at[6], orx.at[row], (z, i, col))
    al_acc[...] = jnp.zeros_like(al_acc)

    wait(wbuf, wsem)
    wait(ini.at[0:3], gr.at[5])

    @pl.loop(0, 4)
    def _(k):
        pieces = [ini[k, p].astype(f32) for p in range(3)]
        invi[k] = frame(*pieces, lax.rem(k, 2), u_ref).astype(bf16)

    @pl.loop(0, 4)
    def _(n):
        lanes = pl.ds(mul(n * PAIR, 128), PAIR)
        for q in range(2):
            at = q * PAIR
            first = jnp.dot(
                invi[2 * q, 0:192], wbuf[at : at + 256, lanes], preferred_element_type=f32
            )
            second = jnp.dot(
                invi[2 * q + 1, 64:256], wbuf[at + 128 : at + 384, lanes], preferred_element_type=f32
            )
            left[at : at + 192, lanes] = first.astype(bf16)
            left[at + 192 : at + 384, lanes] = second.astype(bf16)

    @pl.loop(0, 4)
    def _(q):
        for e in range(2):
            lanes = pl.ds(mul(q * PAIR + e * 128, 128), 256)
            grown = dot0(left[:, lanes], wbuf[:, lanes])
            for p, piece in enumerate(pack(grown, grown + grown.T, e == 0)):
                tbl[2 * q + e, p] = piece

    def arrival(j):
        m = lax.rem(j, 4)
        yy = lax.rem(y + m + lax.div(m, 2) * (5 - 2 * m), 4)
        return lax.rem(xl + lax.div(j, 4), 2) * 4 + yy

    @pl.loop(0, 8)
    def _(j):
        k = arrival(j)

        @pl.when(j > 0)
        def _():
            wait(ino.at[k], orx.at[k])

        product = tbl[k] * ino[k].astype(f32)
        al_acc[...] = al_acc[...] + jnp.sum(product.reshape(24, 8, 128), axis=0)

    reduce_start(1, al_acc[...])

    @pl.loop(0, 8)
    def _(k):
        @pl.when(k == 6)
        def _():
            reduce_middle(1)

        pieces = [ino[k, p].astype(f32) for p in range(3)]
        invo[...] = frame(*pieces, lax.rem(k, 2), u_ref).astype(bf16)
        lanes = pl.ds(mul(lax.div(k, 2) * PAIR + lax.rem(k, 2) * 128, 128), 256)
        for n in range(3):
            rows = pl.ds(n * 256, 256)
            part = jnp.dot(left[rows, lanes], invo[...], preferred_element_type=f32)
            nat[rows, lanes] = nat[rows, lanes] + part

    alignment = total(reduce_end(1))
    factor = jnp.sqrt(TRUST_RADIUS * D * F / alignment)
    out[...] = (nat[...] * factor).astype(bf16)

    wait(tbuf.at[:, LOCAL:], tss.at[0])
    wait(gbuf.at[:, LOCAL:], gss.at[0])
    wait(ro0, fss.at[0])
    for k, recv in ((0, ri0), (1, ri1), (2, ri2), (4, ro1), (5, ro2)):
        wait(recv, nss.at[k])
    for use in range(2):
        wait(ar1.at[use, 0:7], gs.at[use])
        wait(ar2.at[use, 0:15], gs.at[2 + use])
    wait(inp.at[:, 0:48], gs.at[4])
    wait(ini.at[0:3], gs.at[5])
    wait(ino.at[0:7], gs.at[6])


def on_device(tokens, grads, weight_grad):
    dma = pltpu.SemaphoreType.DMA
    any_space = pl.BlockSpec(memory_space=pltpu.HBM)
    vmem = pltpu.VMEM

    def received(net, sub):
        sizes = [24 * sub // 4**s for s in range(3)]
        return [
            vmem((3, 3, n * 2 // 3, 128) if (net, s) in DIRECT else (3, 2, n, 128), f32)
            for s, n in enumerate(sizes)
        ]

    return pl.pallas_call(
        kernel,
        out_shape=jax.ShapeDtypeStruct((ROWS, COLS), bf16),
        in_specs=[any_space] * 3,
        out_specs=pl.BlockSpec(memory_space=vmem),
        scratch_shapes=[
            vmem((IN_PAIRS, 2 * LOCAL, PAIR), bf16),
            vmem((OUT_PAIRS, 2 * LOCAL, PAIR), bf16),
            vmem((ROWS, COLS), bf16),
            vmem((ROWS, COLS), bf16),
            vmem((ROWS, COLS), f32),
            vmem((3, 64 * SUB_IN, 128), f32),
            vmem((3, 64 * SUB_OUT, 128), f32),
            *received(0, SUB_IN),
            vmem((3, 4, 2, 6 * SUB_OUT, 128), f32),
            *received(1, SUB_OUT)[1:],
            vmem((3, 64, 128), f32),
            vmem((4, 3, 64, 128), bf16),
            vmem((8, 3, 64, 128), bf16),
            vmem((4, 256, 256), bf16),
            vmem((256, 256), bf16),
            vmem((8, 3, 64, 128), f32),
            vmem((256, 256), f32),
            vmem((2, 64, 128), f32),
            vmem((8, 128), f32),
            vmem((2, 8, 8, 128), f32),
            vmem((2, 16, 8, 128), f32),
            dma((IN_PAIRS // 2,)),
            dma((OUT_PAIRS // 2,)),
            dma((1,)),
            dma((1,)),
            dma(()),
            dma((6,)),
            dma((3, 7)),
            dma((1,)),
            dma((3, 4, 2)),
            dma((7,)),
            dma((7,)),
            dma((8,)),
        ],
        compiler_params=pltpu.CompilerParams(
            collective_id=0, has_side_effects=True, vmem_limit_bytes=50 * 1024 * 1024
        ),
        name="kfac_step",
    )(tokens, grads, weight_grad)


def solution(mesh):
    every = P(("dp", "row", "col"), None)
    weight = P("row", ("dp", "col"))
    return jax.shard_map(
        on_device, mesh=mesh, in_specs=(every, every, weight), out_specs=weight, check_vma=False
    )
```

```python
import functools
import math

import jax
import jax.numpy as jnp
from jax import lax
from jax.experimental import pallas as pl
from jax.experimental.pallas import tpu as pltpu
from jax.sharding import PartitionSpec as P

D = 6144
F = 24576
BLOCK = 192
TOKENS = 32768
EPSILON = 1e-06
DAMP_ROOT = math.sqrt(0.01)
TRUST_RADIUS = 0.05

PAIR = 2 * BLOCK
LOCAL = 256
IN_PAIRS = 8
OUT_PAIRS = 32
DIRECT = ((0, 1), (0, 2), (1, 2))
RELAY_AT = 4
AHEAD = 8
SUB_IN = 16
SUB_OUT = 64
ROWS = 768
COLS = 1536
MESH = pl.DeviceIdType.MESH
f32 = jnp.float32
bf16 = jnp.bfloat16


def mul(a, n):
    return pl.multiple_of(a, n)


def dot0(a, b):
    return lax.dot_general(a, b, (((0,), (0,)), ((), ())), preferred_element_type=f32)


def pair_pieces(data):
    turned = data.T
    d1 = jnp.dot(turned[0:256], data[:, 0:256], preferred_element_type=f32)
    d2 = jnp.dot(turned[128:384], data[:, 256:384], preferred_element_type=f32)
    low = lax.broadcasted_iota(jnp.int32, (64, 128), 1) < 64
    a = d1[0:128, 0:128]
    mid = d1[128:256, 128:256]
    b = d1[128:192, 0:128]
    even = (jnp.where(low, a[0:64], a[64:128]), jnp.where(low, mid[0:64], a[0:64]), b)
    a2 = d2[128:256]
    b2 = d2[64:128]
    odd = (jnp.where(low, a2[0:64], a2[64:128]), jnp.where(low, a2[64:128], mid[64:128]), b2)
    return even, odd


def pair_trace(even, odd):
    row = lax.broadcasted_iota(jnp.int32, (64, 128), 0)
    lane = lax.broadcasted_iota(jnp.int32, (64, 128), 1)
    first = lane == row
    second = lane == row + 64
    zero = jnp.zeros((64, 128), f32)
    total = jnp.where(first | second, even[0] + odd[0], zero)
    return total + jnp.where(first, even[1], zero) + jnp.where(second, odd[1], zero)


def frame(p0, p1, p2, parity, u_ref):
    low = lax.broadcasted_iota(jnp.int32, (64, 128), 1) < 64
    even = parity == 0
    zero = jnp.zeros((64, 128), f32)
    u_ref[0:64, 0:128] = jnp.where(even, jnp.where(low, p0, p1), zero)
    u_ref[0:64, 128:256] = zero
    u_ref[64:128, 0:128] = jnp.where(low, zero, jnp.where(even, p0, p1))
    u_ref[64:128, 128:256] = jnp.where(even, zero, p2)
    u_ref[128:192, 0:128] = jnp.where(even, p2, zero)
    u_ref[128:192, 128:256] = jnp.where(low, jnp.where(even, p1, p0), zero)
    u_ref[192:256, 0:128] = zero
    u_ref[192:256, 128:256] = jnp.where(even, zero, jnp.where(low, p1, p0))
    u = u_ref[...]
    row = lax.broadcasted_iota(jnp.int32, (256, 256), 0)
    col = lax.broadcasted_iota(jnp.int32, (256, 256), 1)
    same = lax.div(row, 64) == lax.div(col, 64)
    return u + jnp.where(same, 0.0, u.T)


def pack(own, off, even):
    def pick(a, b):
        return (a if even else b) if isinstance(even, bool) else jnp.where(even, a, b)

    low = lax.broadcasted_iota(jnp.int32, (64, 128), 1) < 64
    p0 = jnp.where(
        low,
        pick(own[0:64, 0:128], own[128:192, 128:256]),
        pick(own[64:128, 0:128], own[192:256, 128:256]),
    )
    p1 = jnp.where(
        low,
        pick(own[128:192, 128:256], off[192:256, 128:256]),
        pick(off[0:64, 0:128], own[64:128, 0:128]),
    )
    return p0, p1, pick(off[128:192, 0:128], off[64:128, 128:256])


def newton(p0, p1, p2, parity, shift, u_ref):
    even = parity == 0
    row = lax.broadcasted_iota(jnp.int32, (256, 256), 0)
    col = lax.broadcasted_iota(jnp.int32, (256, 256), 1)
    valid = jnp.where(even, (row < BLOCK).astype(f32), (row >= 64).astype(f32))
    eye = jnp.where(row == col, valid, 0.0)
    matrix = frame(p0, p1, p2, parity, u_ref) + shift * eye
    norm = jnp.sqrt(jnp.sum(jnp.sum(matrix * matrix, axis=1, keepdims=True), axis=0, keepdims=True))
    scale = 1.0 / norm
    dot = functools.partial(jnp.dot, precision=lax.Precision.HIGHEST, preferred_element_type=f32)
    r1 = eye - matrix * scale
    r2 = dot(r1, r1)
    r3 = dot(r1, r2)
    r4 = dot(r2, r2)
    low_sum = eye + r1 + r2 + r3
    inv = scale * (low_sum + dot(low_sum, r4))
    return [piece.astype(bf16) for piece in pack(inv, inv, even)]


def kernel(
    tok, grd, wgt, out,
    tbuf, gbuf, wbuf, left, nat, ai, ao,
    ri0, ri1, ri2, ro0, ro1, ro2,
    inp, ini, ino, invi, invo, tbl, u_ref, tr_acc, al_acc, ar1, ar2,
    tsem, gsem, tss, gss, wsem,
    nss, nsr, fss, fsr, gs, gr, orx,
):
    z = lax.axis_index("dp")
    row = lax.axis_index("row")
    col = lax.axis_index("col")
    xl = lax.div(row, 4)
    y = lax.rem(row, 4)
    xh = lax.div(col, 2)
    c = lax.rem(col, 2)
    x = xh * 2 + xl
    other = 1 - c
    pos = (x, y, z)

    def dev(xx, yy, zz, cc):
        return (zz, lax.rem(xx, 2) * 4 + yy, lax.div(xx, 2) * 2 + cc)

    def shifted(axis, delta):
        p = list(pos)
        p[axis] = lax.rem(p[axis] + delta, 4)
        return dev(*p, c)

    def remote(src, dst, ss, rs, device):
        pltpu.make_async_remote_copy(
            src_ref=src, dst_ref=dst, send_sem=ss, recv_sem=rs, device_id=device, device_id_type=MESH
        ).start()

    def wait(ref, sem):
        pltpu.make_async_copy(ref, ref, sem).wait()

    plane = []
    for j in range(1, 8):
        i = lax.rem(x * 2 + c + j, 8)
        plane.append(dev(lax.div(i, 2), y, z, lax.rem(i, 2)))
    sheet = []
    for j in range(1, 16):
        i = lax.rem(y * 4 + z + j, 16)
        sheet.append(dev(x, lax.div(i, 4), lax.rem(i, 4), c))
    diagonal = [dev(xh * 2 + 1 - xl, lax.rem(y + j, 4), z, c) for j in range(1, 4)]
    x_far, z_far = lax.rem(x + 2, 4), lax.rem(z + 2, 4)
    z_near = z + 1 - 2 * lax.rem(z, 2)
    corners = [dev(x_far, y, z, c), dev(x, y, z_far, c), dev(x_far, y, z_far, c)]
    cousins = [dev(x, y, z, other), dev(x, y, z_near, c), dev(x, y, z_near, other)]

    barrier = pltpu.get_barrier_semaphore()
    peers = plane + sheet + diagonal + [corners[2], cousins[2]]
    for device in peers:
        pl.semaphore_signal(barrier, inc=1, device_id=device, device_id_type=MESH)

    def tok_lanes(i, core):
        return pl.ds(mul((2 * i + core) * PAIR, 128), PAIR)

    def out_place(i):
        n = lax.div(i, 2)
        dx = lax.rem(2 + n, 4)
        dz = lax.rem(2 + n + lax.div(n, 4), 4)
        yh = lax.rem(lax.div(y, 2) + 1 + lax.rem(i, 2), 2)
        return lax.rem(x + dx, 4), yh, lax.rem(z + dz, 4)

    def grd_lanes(i, core):
        xx, yh, zz = out_place(i)
        pair = (zz * 4 + lax.div(xx, 2) * 2 + core) * 4 + lax.rem(xx, 2) * 2 + yh
        return pl.ds(mul(pair * PAIR, 128), PAIR)

    @pl.loop(0, IN_PAIRS)
    def _(i):
        pltpu.make_async_copy(tok.at[:, tok_lanes(i, c)], tbuf.at[i, 0:LOCAL], tsem.at[lax.div(i, 2)]).start()

    @pl.loop(0, OUT_PAIRS)
    def _(i):
        pltpu.make_async_copy(grd.at[:, grd_lanes(i, c)], gbuf.at[i, 0:LOCAL], gsem.at[lax.div(i, 2)]).start()

    pltpu.make_async_copy(wgt, wbuf, wsem).start()

    tr_acc[...] = jnp.zeros_like(tr_acc)
    nat[...] = jnp.zeros_like(nat)

    pl.semaphore_wait(barrier, len(peers))

    partner = dev(x, y, z, other)

    @pl.loop(0, IN_PAIRS)
    def _(i):
        remote(tok.at[:, tok_lanes(i, other)], tbuf.at[i, LOCAL:], tss.at[0], tsem.at[lax.div(i, 2)], partner)

    def swap_out(i):
        remote(grd.at[:, grd_lanes(i, other)], gbuf.at[i, LOCAL:], gss.at[0], gsem.at[lax.div(i, 2)], partner)

    @pl.loop(0, AHEAD)
    def _(i):
        swap_out(i)

    def index(p, xx, yy, zz):
        t = (xx, yy, zz)
        return t[p] * 16 + t[(p + 1) % 3] * 4 + t[(p + 2) % 3]

    def base(p, stage, sub):
        b = 0
        for s in range(stage):
            b = b + pos[(p + s) % 3] * ((16, 4, 1)[s] * sub)
        return b

    class Ring:
        def __init__(self, axis, buf, recv, ss, rs, b, stride, n):
            self.axis, self.buf, self.recv, self.ss, self.rs = axis, buf, recv, ss, rs
            self.b, self.stride, self.n, self.h = b, stride, n, n // 2

        def part(self, step, offset, rows):
            return pl.ds(mul(self.b + lax.rem(pos[self.axis] + step, 4) * self.stride + offset, 8), rows)

        def place(self, direction, kind, offset):
            return self.recv.at[direction, pl.ds(0 if kind == 0 else self.h + offset, self.h)]

        def send(self, direction, kind, step, offset):
            remote(
                self.buf.at[self.part(step, offset, self.h)], self.place(direction, kind, offset),
                self.ss, self.rs[min(kind, 1)], shifted(self.axis, 3 if direction else 1),
            )

        def far(self):
            self.send(0, 0, 2, 0)
            self.send(1, 0, 2, self.h)

        def near(self, direction):
            self.send(direction, 1, 3 if direction else 1, 0 if direction else self.h)

        def issue(self):
            self.far()
            self.near(0)
            self.near(1)

        def relay(self):
            wait(self.recv.at[:, pl.ds(0, self.h)], self.rs[0])
            for direction, step, offset in ((0, 1, 0), (1, 3, self.h)):
                rows = self.part(step, offset, self.h)
                self.buf[rows] = self.buf[rows] + self.recv[direction, 0 : self.h]
                self.send(direction, 2, step, offset)

        def final(self):
            h, n = self.h, self.n
            wait(self.recv.at[:, pl.ds(h, n)], self.rs[1])
            rows = self.part(0, 0, n)
            self.buf[rows] = self.buf[rows] + self.recv[0, h : h + n] + self.recv[1, h : h + n]

    class Direct(Ring):
        def issue(self):
            n = self.n
            for k in (2, 1, 3):
                remote(
                    self.buf.at[self.part(k, 0, n)], self.recv.at[k - 1], self.ss, self.rs[0],
                    shifted(self.axis, k),
                )

        def final(self):
            wait(self.recv, self.rs[0])
            rows = self.part(0, 0, self.n)
            self.buf[rows] = self.buf[rows] + self.recv[0] + self.recv[1] + self.recv[2]

    def whole_ring(net, stage, p):
        sub = (SUB_IN, SUB_OUT)[net]
        n = (16, 4, 1)[stage] * sub
        recv = ((ri0, ri1, ri2), (None, ro1, ro2))[net][stage]
        kind = Direct if (net, stage) in DIRECT else Ring
        place = {(0, 0): 0, (1, 1): 2, (0, 1): 4, (0, 2): 5, (1, 2): 6}[net, stage]
        return kind(
            (p + stage) % 3, (ai, ao)[net].at[p], recv.at[p], nss.at[3 * net + stage], [nsr.at[p, place + k] for k in range(1 if kind is Direct else 2)],
            base(p, stage, sub), n, n,
        )

    def first_ring(p, step):
        second = lax.rem(pos[(p + 1) % 3] + step, 4)
        return Ring(
            p, ao.at[p], ro0.at[p, second], fss.at[0], [fsr.at[p, second, 0], fsr.at[p, second, 1]],
            second * 4 * SUB_OUT, 16 * SUB_OUT, 4 * SUB_OUT,
        )

    @pl.loop(0, IN_PAIRS // 2)
    def _(n):
        for u in range(2):
            swap_out(AHEAD + 2 * n + u)
        done = []
        wait(tbuf.at[pl.ds(2 * n, 2)], tsem.at[n])
        for u in range(2):
            done.append(pair_pieces(tbuf[2 * n + u]))
        tr_acc[1] = tr_acc[1] + (pair_trace(*done[0]) + pair_trace(*done[1]))
        for u, pieces in enumerate(done):
            i = 2 * n + u
            for e in range(2):
                for p in range(3):
                    for q in range(4):
                        xx = q // 2 * 2 + lax.div(i, 4)
                        at = index(p, xx, lax.rem(i, 4), q % 2 * 2 + e) * SUB_IN
                        ai[p, pl.ds(mul(at, SUB_IN), SUB_IN)] = pieces[e][p][q * 16 : q * 16 + 16]

    in_rings = [[whole_ring(0, s, p) for p in range(3)] for s in range(3)]
    out_rings = [None] + [[whole_ring(1, s, p) for p in range(3)] for s in range(1, 3)]
    for p in range(3):
        in_rings[0][p].issue()

    order = (2, 0, 1)

    def advance(rings, stage):
        for p in order:
            rings[stage][p].final()
            rings[stage + 1][p].issue()

    @pl.loop(0, OUT_PAIRS // 2)
    def _(n):
        @pl.when(n == RELAY_AT)
        def _():
            for p in order:
                in_rings[0][p].relay()

        @pl.when(n < (OUT_PAIRS - AHEAD - IN_PAIRS) // 2)
        def _():
            for u in range(2):
                swap_out(AHEAD + IN_PAIRS + 2 * n + u)

        wait(gbuf.at[pl.ds(2 * n, 2)], gsem.at[n])
        done = [pair_pieces(gbuf[2 * n + u]) for u in range(2)]
        tr_acc[0] = tr_acc[0] + (pair_trace(*done[0]) + pair_trace(*done[1]))
        sends = []
        for u, pieces in enumerate(done):
            xx, yh, zz = out_place(2 * n + u)
            for p, e in ((2, 0), (2, 1), (0, 0), (0, 1), (1, 0), (1, 1)):
                place = (xx, 2 * yh + e, zz)
                second, third = place[(p + 1) % 3], place[(p + 2) % 3]
                at = mul((place[p] * 16 + second * 4 + third) * SUB_OUT, SUB_OUT)
                ao[p, pl.ds(at, SUB_OUT)] = pieces[e][p]
                if p < 2:
                    sends.append((p, place[p], second, third, at, SUB_OUT))
                elif e == 0:
                    sends.append((p, place[p], second, third, at, 2 * SUB_OUT))
        for p, first, second, third, at, count in sends:
            d = lax.rem(first - pos[p] + 4, 4)
            h = lax.div(third, 2)
            far = (1 - lax.rem(d, 2)) * lax.div(d, 2)
            go = far + lax.rem(d, 2) * lax.rem(lax.div(d, 2) + h, 2)
            direction = far * h + (1 - far) * (1 - h)
            to = (far * lax.rem(third, 2) + (1 - far) * (2 + third)) * SUB_OUT

            @pl.when(go == 1)
            def _():
                remote(
                    ao.at[p, pl.ds(at, count)],
                    ro0.at[p, second, direction, pl.ds(mul(to, SUB_OUT), count)],
                    fss.at[0], fsr.at[p, second, 1 - far],
                    shifted(p, 1 + 2 * direction),
                )

    def reduce_start(use, value):
        mine = x * 2 + c
        ar1[use, mine] = value
        for device in plane:
            remote(ar1.at[use, mine], ar1.at[use, mine], gs.at[use], gr.at[use], device)

    def reduce_middle(use):
        wait(ar1.at[use, 0:7], gr.at[use])
        mine = y * 4 + z
        ar2[use, mine] = jnp.sum(ar1[use], axis=0)
        for device in sheet:
            remote(ar2.at[use, mine], ar2.at[use, mine], gs.at[2 + use], gr.at[2 + use], device)

    def reduce_end(use):
        wait(ar2.at[use, 0:15], gr.at[2 + use])
        return jnp.sum(ar2[use], axis=0)

    def total(value):
        return jnp.sum(jnp.sum(value, axis=1, keepdims=True), axis=0, keepdims=True)

    t_out = jnp.sum(tr_acc[0].reshape(16, 4, 128), axis=0)
    t_in = jnp.sum(tr_acc[1].reshape(16, 4, 128), axis=0)
    reduce_start(0, jnp.concatenate([t_out, t_in], axis=0))

    for p in order:
        first_ring(p, 2).relay()
    advance(in_rings, 0)
    for t in (1, 3):
        for p in order:
            first_ring(p, t).relay()
    reduce_middle(0)
    for p in order:
        first_ring(p, 2).final()
        out_rings[1][p].far()
    advance(in_rings, 1)
    for p in order:
        first_ring(p, 0).relay()
    for p in order:
        first_ring(p, 1).final()
        out_rings[1][p].near(0)
    for p in order:
        first_ring(p, 3).final()
        out_rings[1][p].near(1)
    for p in order:
        out_rings[1][p].relay()
    for p in order:
        in_rings[2][p].final()

    quarter = pl.ds(mul((xh * 2 + lax.div(z, 2)) * SUB_IN, SUB_IN), SUB_IN)
    for p in range(3):
        inp[p, quarter] = ai[p, pl.ds(mul(index(p, x, y, z) * SUB_IN, SUB_IN), SUB_IN)]
    for device in reversed(corners):
        remote(inp.at[:, quarter], inp.at[:, quarter], gs.at[4], gr.at[4], device)

    traces = reduce_end(0)
    inverse_count = 1.0 / TOKENS
    trace_out = total(traces[0:4]) * inverse_count
    trace_in = total(traces[4:8]) * inverse_count
    ratio = jnp.sqrt((trace_in / D + EPSILON) / (trace_out / F + EPSILON))
    for p in order:
        first_ring(p, 0).final()
    advance(out_rings, 1)
    wait(inp.at[:, 0:48], gr.at[4])
    slot = c * 2 + lax.rem(z, 2)
    mine = [inp[p] * inverse_count for p in range(3)]
    for p, piece in enumerate(newton(*mine, lax.rem(z, 2), ratio * DAMP_ROOT, u_ref)):
        ini[slot, p] = piece
    for device in reversed(cousins):
        remote(ini.at[slot], ini.at[slot], gs.at[5], gr.at[5], device)

    for p in order:
        out_rings[2][p].final()

    own = [
        ao[p, pl.ds(mul(index(p, x, y, z) * SUB_OUT, SUB_OUT), SUB_OUT)] * inverse_count for p in range(3)
    ]
    for p, piece in enumerate(newton(*own, lax.rem(y, 2), DAMP_ROOT / ratio, u_ref)):
        ino[row, p] = piece
    for dx, dy in ((1, 2), (1, 1), (1, 3), (0, 2), (1, 0), (0, 1), (0, 3)):
        i = lax.rem(xl + dx, 2) * 4 + lax.rem(y + dy, 4)
        remote(ino.at[row], ino.at[row], gs.at[6], orx.at[row], (z, i, col))
    al_acc[...] = jnp.zeros_like(al_acc)

    wait(wbuf, wsem)
    wait(ini.at[0:3], gr.at[5])

    @pl.loop(0, 4)
    def _(k):
        pieces = [ini[k, p].astype(f32) for p in range(3)]
        invi[k] = frame(*pieces, lax.rem(k, 2), u_ref).astype(bf16)

    @pl.loop(0, 4)
    def _(n):
        lanes = pl.ds(mul(n * PAIR, 128), PAIR)
        for q in range(2):
            at = q * PAIR
            first = jnp.dot(
                invi[2 * q, 0:192], wbuf[at : at + 256, lanes], preferred_element_type=f32
            )
            second = jnp.dot(
                invi[2 * q + 1, 64:256], wbuf[at + 128 : at + 384, lanes], preferred_element_type=f32
            )
            left[at : at + 192, lanes] = first.astype(bf16)
            left[at + 192 : at + 384, lanes] = second.astype(bf16)

    @pl.loop(0, 4)
    def _(q):
        for e in range(2):
            lanes = pl.ds(mul(q * PAIR + e * 128, 128), 256)
            grown = dot0(left[:, lanes], wbuf[:, lanes])
            for p, piece in enumerate(pack(grown, grown + grown.T, e == 0)):
                tbl[2 * q + e, p] = piece

    def arrival(j):
        m = lax.rem(j, 4)
        yy = lax.rem(y + m + lax.div(m, 2) * (5 - 2 * m), 4)
        return lax.rem(xl + lax.div(j, 4), 2) * 4 + yy

    @pl.loop(0, 8)
    def _(j):
        k = arrival(j)

        @pl.when(j > 0)
        def _():
            wait(ino.at[k], orx.at[k])

        product = tbl[k] * ino[k].astype(f32)
        al_acc[...] = al_acc[...] + jnp.sum(product.reshape(24, 8, 128), axis=0)

    reduce_start(1, al_acc[...])

    @pl.loop(0, 8)
    def _(k):
        @pl.when(k == 6)
        def _():
            reduce_middle(1)

        pieces = [ino[k, p].astype(f32) for p in range(3)]
        invo[...] = frame(*pieces, lax.rem(k, 2), u_ref).astype(bf16)
        lanes = pl.ds(mul(lax.div(k, 2) * PAIR + lax.rem(k, 2) * 128, 128), 256)
        for n in range(3):
            rows = pl.ds(n * 256, 256)
            part = jnp.dot(left[rows, lanes], invo[...], preferred_element_type=f32)
            nat[rows, lanes] = nat[rows, lanes] + part

    alignment = total(reduce_end(1))
    factor = jnp.sqrt(TRUST_RADIUS * D * F / alignment)
    out[...] = (nat[...] * factor).astype(bf16)

    wait(tbuf.at[:, LOCAL:], tss.at[0])
    wait(gbuf.at[:, LOCAL:], gss.at[0])
    wait(ro0, fss.at[0])
    for k, recv in ((0, ri0), (1, ri1), (2, ri2), (4, ro1), (5, ro2)):
        wait(recv, nss.at[k])
    for use in range(2):
        wait(ar1.at[use, 0:7], gs.at[use])
        wait(ar2.at[use, 0:15], gs.at[2 + use])
    wait(inp.at[:, 0:48], gs.at[4])
    wait(ini.at[0:3], gs.at[5])
    wait(ino.at[0:7], gs.at[6])


def on_device(tokens, grads, weight_grad):
    dma = pltpu.SemaphoreType.DMA
    any_space = pl.BlockSpec(memory_space=pltpu.HBM)
    vmem = pltpu.VMEM

    def received(net, sub):
        sizes = [24 * sub // 4**s for s in range(3)]
        return [
            vmem((3, 3, n * 2 // 3, 128) if (net, s) in DIRECT else (3, 2, n, 128), f32)
            for s, n in enumerate(sizes)
        ]

    return pl.pallas_call(
        kernel,
        out_shape=jax.ShapeDtypeStruct((ROWS, COLS), bf16),
        in_specs=[any_space] * 3,
        out_specs=pl.BlockSpec(memory_space=vmem),
        scratch_shapes=[
            vmem((IN_PAIRS, 2 * LOCAL, PAIR), bf16),
            vmem((OUT_PAIRS, 2 * LOCAL, PAIR), bf16),
            vmem((ROWS, COLS), bf16),
            vmem((ROWS, COLS), bf16),
            vmem((ROWS, COLS), f32),
            vmem((3, 64 * SUB_IN, 128), f32),
            vmem((3, 64 * SUB_OUT, 128), f32),
            *received(0, SUB_IN),
            vmem((3, 4, 2, 6 * SUB_OUT, 128), f32),
            *received(1, SUB_OUT)[1:],
            vmem((3, 64, 128), f32),
            vmem((4, 3, 64, 128), bf16),
            vmem((8, 3, 64, 128), bf16),
            vmem((4, 256, 256), bf16),
            vmem((256, 256), bf16),
            vmem((8, 3, 64, 128), f32),
            vmem((256, 256), f32),
            vmem((2, 64, 128), f32),
            vmem((8, 128), f32),
            vmem((2, 8, 8, 128), f32),
            vmem((2, 16, 8, 128), f32),
            dma((IN_PAIRS // 2,)),
            dma((OUT_PAIRS // 2,)),
            dma((1,)),
            dma((1,)),
            dma(()),
            dma((6,)),
            dma((3, 7)),
            dma((1,)),
            dma((3, 4, 2)),
            dma((7,)),
            dma((7,)),
            dma((8,)),
        ],
        compiler_params=pltpu.CompilerParams(
            collective_id=0, has_side_effects=True, vmem_limit_bytes=50 * 1024 * 1024
        ),
        name="kfac_step",
    )(tokens, grads, weight_grad)


def solution(mesh):
    every = P(("dp", "row", "col"), None)
    weight = P("row", ("dp", "col"))
    return jax.shard_map(
        on_device, mesh=mesh, in_specs=(every, every, weight), out_specs=weight, check_vma=False
    )
```

```python
import functools
import math

import jax
import jax.numpy as jnp
from jax import lax
from jax.experimental import pallas as pl
from jax.experimental.pallas import tpu as pltpu
from jax.sharding import PartitionSpec as P

D = 6144
F = 24576
BLOCK = 192
TOKENS = 32768
EPSILON = 1e-06
DAMP_ROOT = math.sqrt(0.01)
TRUST_RADIUS = 0.05

PAIR = 2 * BLOCK
LOCAL = 256
IN_PAIRS = 8
OUT_PAIRS = 32
DIRECT = ((0, 1), (0, 2), (1, 2))
RELAY_AT = 7
AHEAD = 8
SUB_IN = 16
SUB_OUT = 64
ROWS = 768
COLS = 1536
MESH = pl.DeviceIdType.MESH


def farthest(steps):
    return -sum(min(d, 4 - d) for d in steps)


f32 = jnp.float32
bf16 = jnp.bfloat16


def mul(a, n):
    return pl.multiple_of(a, n)


def dot0(a, b):
    return lax.dot_general(a, b, (((0,), (0,)), ((), ())), preferred_element_type=f32)


def pair_pieces(data):
    turned = data.T
    d1 = jnp.dot(turned[0:256], data[:, 0:256], preferred_element_type=f32)
    d2 = jnp.dot(turned[128:384], data[:, 256:384], preferred_element_type=f32)
    low = lax.broadcasted_iota(jnp.int32, (64, 128), 1) < 64
    a = d1[0:128, 0:128]
    mid = d1[128:256, 128:256]
    b = d1[128:192, 0:128]
    even = (jnp.where(low, a[0:64], a[64:128]), jnp.where(low, mid[0:64], a[0:64]), b)
    a2 = d2[128:256]
    b2 = d2[64:128]
    odd = (jnp.where(low, a2[0:64], a2[64:128]), jnp.where(low, a2[64:128], mid[64:128]), b2)
    return even, odd


def pair_trace(even, odd):
    row = lax.broadcasted_iota(jnp.int32, (64, 128), 0)
    lane = lax.broadcasted_iota(jnp.int32, (64, 128), 1)
    first = lane == row
    second = lane == row + 64
    zero = jnp.zeros((64, 128), f32)
    total = jnp.where(first | second, even[0] + odd[0], zero)
    return total + jnp.where(first, even[1], zero) + jnp.where(second, odd[1], zero)


def frame(p0, p1, p2, parity, u_ref):
    low = lax.broadcasted_iota(jnp.int32, (64, 128), 1) < 64
    even = parity == 0
    zero = jnp.zeros((64, 128), f32)
    u_ref[0:64, 0:128] = jnp.where(even, jnp.where(low, p0, p1), zero)
    u_ref[0:64, 128:256] = zero
    u_ref[64:128, 0:128] = jnp.where(low, zero, jnp.where(even, p0, p1))
    u_ref[64:128, 128:256] = jnp.where(even, zero, p2)
    u_ref[128:192, 0:128] = jnp.where(even, p2, zero)
    u_ref[128:192, 128:256] = jnp.where(low, jnp.where(even, p1, p0), zero)
    u_ref[192:256, 0:128] = zero
    u_ref[192:256, 128:256] = jnp.where(even, zero, jnp.where(low, p1, p0))
    u = u_ref[...]
    row = lax.broadcasted_iota(jnp.int32, (256, 256), 0)
    col = lax.broadcasted_iota(jnp.int32, (256, 256), 1)
    same = lax.div(row, 64) == lax.div(col, 64)
    return u + jnp.where(same, 0.0, u.T)


def pack(own, off, even):
    def pick(a, b):
        return (a if even else b) if isinstance(even, bool) else jnp.where(even, a, b)

    low = lax.broadcasted_iota(jnp.int32, (64, 128), 1) < 64
    p0 = jnp.where(
        low,
        pick(own[0:64, 0:128], own[128:192, 128:256]),
        pick(own[64:128, 0:128], own[192:256, 128:256]),
    )
    p1 = jnp.where(
        low,
        pick(own[128:192, 128:256], off[192:256, 128:256]),
        pick(off[0:64, 0:128], own[64:128, 0:128]),
    )
    return p0, p1, pick(off[128:192, 0:128], off[64:128, 128:256])


def newton(p0, p1, p2, parity, shift, u_ref):
    even = parity == 0
    row = lax.broadcasted_iota(jnp.int32, (256, 256), 0)
    col = lax.broadcasted_iota(jnp.int32, (256, 256), 1)
    valid = jnp.where(even, (row < BLOCK).astype(f32), (row >= 64).astype(f32))
    eye = jnp.where(row == col, valid, 0.0)
    matrix = frame(p0, p1, p2, parity, u_ref) + shift * eye
    norm = jnp.sqrt(jnp.sum(jnp.sum(matrix * matrix, axis=1, keepdims=True), axis=0, keepdims=True))
    scale = 1.0 / norm
    dot = functools.partial(jnp.dot, precision=lax.Precision.HIGHEST, preferred_element_type=f32)
    r1 = eye - matrix * scale
    r2 = dot(r1, r1)
    r3 = dot(r1, r2)
    r4 = dot(r2, r2)
    low_sum = eye + r1 + r2 + r3
    inv = scale * (low_sum + dot(low_sum, r4))
    return [piece.astype(bf16) for piece in pack(inv, inv, even)]


def kernel(
    tok, grd, wgt, out,
    tbuf, gbuf, wbuf, left, nat, ai, ao,
    ri0, ri1, ri2, ro0, ro1, ro2,
    inp, ini, ino, invi, invo, tbl, u_ref, tr_acc, al_acc, ar1, ar2,
    tsem, gsem, tss, gss, wsem,
    nss, nsr, fss, fsr, gs, gr,
):
    z = lax.axis_index("dp")
    row = lax.axis_index("row")
    col = lax.axis_index("col")
    xl = lax.div(row, 4)
    y = lax.rem(row, 4)
    xh = lax.div(col, 2)
    c = lax.rem(col, 2)
    x = xh * 2 + xl
    other = 1 - c
    pos = (x, y, z)

    def dev(xx, yy, zz, cc):
        return (zz, lax.rem(xx, 2) * 4 + yy, lax.div(xx, 2) * 2 + cc)

    def shifted(axis, delta):
        p = list(pos)
        p[axis] = lax.rem(p[axis] + delta, 4)
        return dev(*p, c)

    def remote(src, dst, ss, rs, device):
        pltpu.make_async_remote_copy(
            src_ref=src, dst_ref=dst, send_sem=ss, recv_sem=rs, device_id=device, device_id_type=MESH
        ).start()

    def wait(ref, sem):
        pltpu.make_async_copy(ref, ref, sem).wait()

    plane = []
    for dx, dc in sorted(((j // 2, j % 2) for j in range(1, 8)), key=farthest):
        plane.append(dev(lax.rem(x + dx, 4), y, z, lax.rem(c + dc, 2)))
    sheet = []
    for dy, dz in sorted(((j // 4, j % 4) for j in range(1, 16)), key=farthest):
        sheet.append(dev(x, lax.rem(y + dy, 4), lax.rem(z + dz, 4), c))
    diagonal = [dev(xh * 2 + 1 - xl, lax.rem(y + j, 4), z, c) for j in range(1, 4)]
    x_far, z_far = lax.rem(x + 2, 4), lax.rem(z + 2, 4)
    z_near = z + 1 - 2 * lax.rem(z, 2)
    corners = [dev(x_far, y, z, c), dev(x, y, z_far, c), dev(x_far, y, z_far, c)]
    cousins = [dev(x, y, z, other), dev(x, y, z_near, c), dev(x, y, z_near, other)]

    barrier = pltpu.get_barrier_semaphore()
    peers = plane + sheet + diagonal + [corners[2], cousins[2]]
    for device in peers:
        pl.semaphore_signal(barrier, inc=1, device_id=device, device_id_type=MESH)

    def tok_lanes(i, core):
        return pl.ds(mul((2 * i + core) * PAIR, 128), PAIR)

    def out_place(i):
        n = lax.div(i, 2)
        dx = lax.rem(2 + n, 4)
        dz = lax.rem(2 + n + lax.div(n, 4), 4)
        yh = lax.rem(lax.div(y, 2) + 1 + lax.rem(i, 2), 2)
        return lax.rem(x + dx, 4), yh, lax.rem(z + dz, 4)

    def grd_lanes(i, core):
        xx, yh, zz = out_place(i)
        pair = (zz * 4 + lax.div(xx, 2) * 2 + core) * 4 + lax.rem(xx, 2) * 2 + yh
        return pl.ds(mul(pair * PAIR, 128), PAIR)

    @pl.loop(0, IN_PAIRS)
    def _(i):
        pltpu.make_async_copy(tok.at[:, tok_lanes(i, c)], tbuf.at[i, 0:LOCAL], tsem.at[lax.div(i, 2)]).start()

    @pl.loop(0, OUT_PAIRS)
    def _(i):
        pltpu.make_async_copy(grd.at[:, grd_lanes(i, c)], gbuf.at[i, 0:LOCAL], gsem.at[lax.div(i, 2)]).start()

    pltpu.make_async_copy(wgt, wbuf, wsem).start()

    tr_acc[...] = jnp.zeros_like(tr_acc)
    nat[...] = jnp.zeros_like(nat)

    pl.semaphore_wait(barrier, len(peers))

    partner = dev(x, y, z, other)

    @pl.loop(0, IN_PAIRS)
    def _(i):
        remote(tok.at[:, tok_lanes(i, other)], tbuf.at[i, LOCAL:], tss.at[0], tsem.at[lax.div(i, 2)], partner)

    def swap_out(i):
        remote(grd.at[:, grd_lanes(i, other)], gbuf.at[i, LOCAL:], gss.at[0], gsem.at[lax.div(i, 2)], partner)

    @pl.loop(0, AHEAD)
    def _(i):
        swap_out(i)

    def index(p, xx, yy, zz):
        t = (xx, yy, zz)
        return t[p] * 16 + t[(p + 1) % 3] * 4 + t[(p + 2) % 3]

    def base(p, stage, sub):
        b = 0
        for s in range(stage):
            b = b + pos[(p + s) % 3] * ((16, 4, 1)[s] * sub)
        return b

    class Ring:
        def __init__(self, axis, buf, recv, ss, rs, b, stride, n):
            self.axis, self.buf, self.recv, self.ss, self.rs = axis, buf, recv, ss, rs
            self.b, self.stride, self.n, self.h = b, stride, n, n // 2

        def part(self, step, offset, rows):
            return pl.ds(mul(self.b + lax.rem(pos[self.axis] + step, 4) * self.stride + offset, 8), rows)

        def place(self, direction, kind, offset):
            return self.recv.at[direction, pl.ds(0 if kind == 0 else self.h + offset, self.h)]

        def send(self, direction, kind, step, offset):
            remote(
                self.buf.at[self.part(step, offset, self.h)], self.place(direction, kind, offset),
                self.ss, self.rs[min(kind, 1)], shifted(self.axis, 3 if direction else 1),
            )

        def far(self):
            self.send(0, 0, 2, 0)
            self.send(1, 0, 2, self.h)

        def near(self, direction):
            self.send(direction, 1, 3 if direction else 1, 0 if direction else self.h)

        def issue(self):
            self.far()
            self.near(0)
            self.near(1)

        def relay(self):
            wait(self.recv.at[:, pl.ds(0, self.h)], self.rs[0])
            for direction, step, offset in ((0, 1, 0), (1, 3, self.h)):
                rows = self.part(step, offset, self.h)
                self.buf[rows] = self.buf[rows] + self.recv[direction, 0 : self.h]
                self.send(direction, 2, step, offset)

        def final(self):
            h, n = self.h, self.n
            wait(self.recv.at[:, pl.ds(h, n)], self.rs[1])
            rows = self.part(0, 0, n)
            self.buf[rows] = self.buf[rows] + self.recv[0, h : h + n] + self.recv[1, h : h + n]

    class Direct(Ring):
        def issue(self):
            n = self.n
            for k in (2, 1, 3):
                remote(
                    self.buf.at[self.part(k, 0, n)], self.recv.at[k - 1], self.ss, self.rs[0],
                    shifted(self.axis, k),
                )

        def final(self):
            wait(self.recv, self.rs[0])
            rows = self.part(0, 0, self.n)
            self.buf[rows] = self.buf[rows] + self.recv[0] + self.recv[1] + self.recv[2]

    def whole_ring(net, stage, p):
        sub = (SUB_IN, SUB_OUT)[net]
        n = (16, 4, 1)[stage] * sub
        recv = ((ri0, ri1, ri2), (None, ro1, ro2))[net][stage]
        kind = Direct if (net, stage) in DIRECT else Ring
        place = {(0, 0): 0, (1, 1): 2, (0, 1): 4, (0, 2): 5, (1, 2): 6}[net, stage]
        return kind(
            (p + stage) % 3, (ai, ao)[net].at[p], recv.at[p], nss.at[3 * net + stage], [nsr.at[p, place + k] for k in range(1 if kind is Direct else 2)],
            base(p, stage, sub), n, n,
        )

    def first_ring(p, step):
        second = lax.rem(pos[(p + 1) % 3] + step, 4)
        return Ring(
            p, ao.at[p], ro0.at[p, second], fss.at[0], [fsr.at[p, second, 0], fsr.at[p, second, 1]],
            second * 4 * SUB_OUT, 16 * SUB_OUT, 4 * SUB_OUT,
        )

    @pl.loop(0, IN_PAIRS // 2)
    def _(n):
        for u in range(2):
            swap_out(AHEAD + 2 * n + u)
        done = []
        wait(tbuf.at[pl.ds(2 * n, 2)], tsem.at[n])
        for u in range(2):
            done.append(pair_pieces(tbuf[2 * n + u]))
        tr_acc[1] = tr_acc[1] + (pair_trace(*done[0]) + pair_trace(*done[1]))
        for u, pieces in enumerate(done):
            i = 2 * n + u
            for e in range(2):
                for p in range(3):
                    for q in range(4):
                        xx = q // 2 * 2 + lax.div(i, 4)
                        at = index(p, xx, lax.rem(i, 4), q % 2 * 2 + e) * SUB_IN
                        ai[p, pl.ds(mul(at, SUB_IN), SUB_IN)] = pieces[e][p][q * 16 : q * 16 + 16]

    in_rings = [[whole_ring(0, s, p) for p in range(3)] for s in range(3)]
    out_rings = [None] + [[whole_ring(1, s, p) for p in range(3)] for s in range(1, 3)]
    for p in range(3):
        in_rings[0][p].issue()

    order = (2, 0, 1)

    def advance(rings, stage):
        for p in order:
            rings[stage][p].final()
            rings[stage + 1][p].issue()

    @pl.loop(0, OUT_PAIRS // 2)
    def _(n):
        @pl.when(n == RELAY_AT)
        def _():
            for p in order:
                in_rings[0][p].relay()

        @pl.when(n < (OUT_PAIRS - AHEAD - IN_PAIRS) // 2)
        def _():
            for u in range(2):
                swap_out(AHEAD + IN_PAIRS + 2 * n + u)

        wait(gbuf.at[pl.ds(2 * n, 2)], gsem.at[n])
        done = [pair_pieces(gbuf[2 * n + u]) for u in range(2)]
        tr_acc[0] = tr_acc[0] + (pair_trace(*done[0]) + pair_trace(*done[1]))
        sends = []
        for u, pieces in enumerate(done):
            xx, yh, zz = out_place(2 * n + u)
            for p, e in ((2, 0), (2, 1), (0, 0), (0, 1), (1, 0), (1, 1)):
                place = (xx, 2 * yh + e, zz)
                second, third = place[(p + 1) % 3], place[(p + 2) % 3]
                at = mul((place[p] * 16 + second * 4 + third) * SUB_OUT, SUB_OUT)
                ao[p, pl.ds(at, SUB_OUT)] = pieces[e][p]
                if p < 2:
                    sends.append((p, place[p], second, third, at, SUB_OUT))
                elif e == 0:
                    sends.append((p, place[p], second, third, at, 2 * SUB_OUT))
        for p, first, second, third, at, count in sends:
            d = lax.rem(first - pos[p] + 4, 4)
            h = lax.div(third, 2)
            far = (1 - lax.rem(d, 2)) * lax.div(d, 2)
            go = far + lax.rem(d, 2) * lax.rem(lax.div(d, 2) + h, 2)
            direction = far * h + (1 - far) * (1 - h)
            to = (far * lax.rem(third, 2) + (1 - far) * (2 + third)) * SUB_OUT

            @pl.when(go == 1)
            def _():
                remote(
                    ao.at[p, pl.ds(at, count)],
                    ro0.at[p, second, direction, pl.ds(mul(to, SUB_OUT), count)],
                    fss.at[0], fsr.at[p, second, 1 - far],
                    shifted(p, 1 + 2 * direction),
                )

    def reduce_start(use, value):
        mine = x * 2 + c
        ar1[use, mine] = value
        for device in plane:
            remote(ar1.at[use, mine], ar1.at[use, mine], gs.at[use], gr.at[use], device)

    def reduce_middle(use):
        wait(ar1.at[use, 0:7], gr.at[use])
        mine = y * 4 + z
        ar2[use, mine] = jnp.sum(ar1[use], axis=0)
        for device in sheet:
            remote(ar2.at[use, mine], ar2.at[use, mine], gs.at[2 + use], gr.at[2 + use], device)

    def reduce_end(use):
        wait(ar2.at[use, 0:15], gr.at[2 + use])
        return jnp.sum(ar2[use], axis=0)

    def total(value):
        return jnp.sum(jnp.sum(value, axis=1, keepdims=True), axis=0, keepdims=True)

    t_out = jnp.sum(tr_acc[0].reshape(16, 4, 128), axis=0)
    t_in = jnp.sum(tr_acc[1].reshape(16, 4, 128), axis=0)
    reduce_start(0, jnp.concatenate([t_out, t_in], axis=0))

    for p in order:
        first_ring(p, 2).relay()
    advance(in_rings, 0)
    for t in (1, 3):
        for p in order:
            first_ring(p, t).relay()
    reduce_middle(0)
    for p in order:
        first_ring(p, 2).final()
        out_rings[1][p].far()
    advance(in_rings, 1)
    for p in order:
        first_ring(p, 0).relay()
    for p in order:
        first_ring(p, 1).final()
        out_rings[1][p].near(0)
    for p in order:
        first_ring(p, 3).final()
        out_rings[1][p].near(1)
    for p in order:
        out_rings[1][p].relay()
    for p in order:
        in_rings[2][p].final()

    quarter = pl.ds(mul((xh * 2 + lax.div(z, 2)) * SUB_IN, SUB_IN), SUB_IN)
    for p in range(3):
        inp[p, quarter] = ai[p, pl.ds(mul(index(p, x, y, z) * SUB_IN, SUB_IN), SUB_IN)]
    for device in reversed(corners):
        remote(inp.at[:, quarter], inp.at[:, quarter], gs.at[4], gr.at[4], device)

    traces = reduce_end(0)
    inverse_count = 1.0 / TOKENS
    trace_out = total(traces[0:4]) * inverse_count
    trace_in = total(traces[4:8]) * inverse_count
    ratio = jnp.sqrt((trace_in / D + EPSILON) / (trace_out / F + EPSILON))
    for p in order:
        first_ring(p, 0).final()
    advance(out_rings, 1)
    wait(inp.at[:, 0:48], gr.at[4])
    slot = c * 2 + lax.rem(z, 2)
    mine = [inp[p] * inverse_count for p in range(3)]
    for p, piece in enumerate(newton(*mine, lax.rem(z, 2), ratio * DAMP_ROOT, u_ref)):
        ini[slot, p] = piece
    for device in reversed(cousins):
        remote(ini.at[slot], ini.at[slot], gs.at[5], gr.at[5], device)

    for p in order:
        out_rings[2][p].final()

    own = [
        ao[p, pl.ds(mul(index(p, x, y, z) * SUB_OUT, SUB_OUT), SUB_OUT)] * inverse_count for p in range(3)
    ]
    for p, piece in enumerate(newton(*own, lax.rem(y, 2), DAMP_ROOT / ratio, u_ref)):
        ino[row, p] = piece
    for dx, dy in ((1, 2), (1, 1), (1, 3), (0, 2), (1, 0), (0, 1), (0, 3)):
        i = lax.rem(xl + dx, 2) * 4 + lax.rem(y + dy, 4)
        remote(ino.at[row], ino.at[row], gs.at[6], gr.at[6], (z, i, col))
    al_acc[...] = jnp.zeros_like(al_acc)

    wait(wbuf, wsem)
    wait(ini.at[0:3], gr.at[5])

    @pl.loop(0, 4)
    def _(k):
        pieces = [ini[k, p].astype(f32) for p in range(3)]
        invi[k] = frame(*pieces, lax.rem(k, 2), u_ref).astype(bf16)

    @pl.loop(0, 4)
    def _(n):
        lanes = pl.ds(mul(n * PAIR, 128), PAIR)
        for q in range(2):
            at = q * PAIR
            first = jnp.dot(
                invi[2 * q, 0:192], wbuf[at : at + 256, lanes], preferred_element_type=f32
            )
            second = jnp.dot(
                invi[2 * q + 1, 64:256], wbuf[at + 128 : at + 384, lanes], preferred_element_type=f32
            )
            left[at : at + 192, lanes] = first.astype(bf16)
            left[at + 192 : at + 384, lanes] = second.astype(bf16)

    @pl.loop(0, 4)
    def _(q):
        for e in range(2):
            lanes = pl.ds(mul(q * PAIR + e * 128, 128), 256)
            grown = dot0(left[:, lanes], wbuf[:, lanes])
            for p, piece in enumerate(pack(grown, grown + grown.T, e == 0)):
                tbl[2 * q + e, p] = piece

    wait(ino.at[0:7], gr.at[6])

    @pl.loop(0, 8)
    def _(k):
        product = tbl[k] * ino[k].astype(f32)
        al_acc[...] = al_acc[...] + jnp.sum(product.reshape(24, 8, 128), axis=0)

    reduce_start(1, al_acc[...])

    @pl.loop(0, 8)
    def _(k):
        @pl.when(k == 6)
        def _():
            reduce_middle(1)

        pieces = [ino[k, p].astype(f32) for p in range(3)]
        invo[...] = frame(*pieces, lax.rem(k, 2), u_ref).astype(bf16)
        lanes = pl.ds(mul(lax.div(k, 2) * PAIR + lax.rem(k, 2) * 128, 128), 256)
        for n in range(3):
            rows = pl.ds(n * 256, 256)
            part = jnp.dot(left[rows, lanes], invo[...], preferred_element_type=f32)
            nat[rows, lanes] = nat[rows, lanes] + part

    alignment = total(reduce_end(1))
    factor = jnp.sqrt(TRUST_RADIUS * D * F / alignment)
    out[...] = (nat[...] * factor).astype(bf16)

    wait(tbuf.at[:, LOCAL:], tss.at[0])
    wait(gbuf.at[:, LOCAL:], gss.at[0])
    wait(ro0, fss.at[0])
    for k, recv in ((0, ri0), (1, ri1), (2, ri2), (4, ro1), (5, ro2)):
        wait(recv, nss.at[k])
    for use in range(2):
        wait(ar1.at[use, 0:7], gs.at[use])
        wait(ar2.at[use, 0:15], gs.at[2 + use])
    wait(inp.at[:, 0:48], gs.at[4])
    wait(ini.at[0:3], gs.at[5])
    wait(ino.at[0:7], gs.at[6])


def on_device(tokens, grads, weight_grad):
    dma = pltpu.SemaphoreType.DMA
    any_space = pl.BlockSpec(memory_space=pltpu.HBM)
    vmem = pltpu.VMEM

    def received(net, sub):
        sizes = [24 * sub // 4**s for s in range(3)]
        return [
            vmem((3, 3, n * 2 // 3, 128) if (net, s) in DIRECT else (3, 2, n, 128), f32)
            for s, n in enumerate(sizes)
        ]

    return pl.pallas_call(
        kernel,
        out_shape=jax.ShapeDtypeStruct((ROWS, COLS), bf16),
        in_specs=[any_space] * 3,
        out_specs=pl.BlockSpec(memory_space=vmem),
        scratch_shapes=[
            vmem((IN_PAIRS, 2 * LOCAL, PAIR), bf16),
            vmem((OUT_PAIRS, 2 * LOCAL, PAIR), bf16),
            vmem((ROWS, COLS), bf16),
            vmem((ROWS, COLS), bf16),
            vmem((ROWS, COLS), f32),
            vmem((3, 64 * SUB_IN, 128), f32),
            vmem((3, 64 * SUB_OUT, 128), f32),
            *received(0, SUB_IN),
            vmem((3, 4, 2, 6 * SUB_OUT, 128), f32),
            *received(1, SUB_OUT)[1:],
            vmem((3, 64, 128), f32),
            vmem((4, 3, 64, 128), bf16),
            vmem((8, 3, 64, 128), bf16),
            vmem((4, 256, 256), bf16),
            vmem((256, 256), bf16),
            vmem((8, 3, 64, 128), f32),
            vmem((256, 256), f32),
            vmem((2, 64, 128), f32),
            vmem((8, 128), f32),
            vmem((2, 8, 8, 128), f32),
            vmem((2, 16, 8, 128), f32),
            dma((IN_PAIRS // 2,)),
            dma((OUT_PAIRS // 2,)),
            dma((1,)),
            dma((1,)),
            dma(()),
            dma((6,)),
            dma((3, 7)),
            dma((1,)),
            dma((3, 4, 2)),
            dma((7,)),
            dma((7,)),
        ],
        compiler_params=pltpu.CompilerParams(
            collective_id=0, has_side_effects=True, vmem_limit_bytes=50 * 1024 * 1024
        ),
        name="kfac_step",
    )(tokens, grads, weight_grad)


def solution(mesh):
    every = P(("dp", "row", "col"), None)
    weight = P("row", ("dp", "col"))
    return jax.shard_map(
        on_device, mesh=mesh, in_specs=(every, every, weight), out_specs=weight, check_vma=False
    )
```
